128 devices in a mesh: half: 2 (over core), ep: 64 (over z, x, y).
Axes of the slice: x: 4, y: 4, z: 4, core: 2. Of those that a mesh axis runs over, the one named last changes fastest.
Arguments:
- activations: bfloat16 [2, 28672, 2048], P('half', 'ep'), may hold values from -6 to 6
- routes: int32 [2, 28672, 1], P('half', 'ep'), may hold values from 0 to 63; in each aligned block of 448 rows (0 to 447, 448 to 895, ..., all dimensions but the last counted through in order) at most 14 rows name the same one
- blocks: int32 [2, 64], P('half'), may hold values from 1 to 7, as said below
- row_scale: bfloat16 [2, 28672], P('half', 'ep'), may hold values from -4 to 4
- gate_up: bfloat16 [64, 2048, 1536], P('ep'), may hold values from -0.125 to 0.125
- down_weight: bfloat16 [64, 768, 2048], P('ep'), may hold values from -0.21875 to 0.21875
- slot_map: int32 [64], replicated, may hold values from 0 to 63
Outputs:
- rows_out: bfloat16 [2, 28672, 2048], P('half', 'ep')
The draws below stay inside these ranges and needn't reach their ends.
Inputs may be any that keep to these rules, and one draw needn't show every extreme that they name: `routes`: among the rows of one device, no destination appears more than 14 times, and some destination appears exactly 14 times. In each group some destination has exactly 7 blocks.
All inputs are finite; a program needn't handle non-finite values.
Results may differ from the reference program's by a relative error of at most 0.0099.
Values may be sent and summed in bfloat16 or wider, within the bound.
No kernel may reach another device: no remote copies, remote signals or barrier semaphores. Data moves between devices by JAX's collectives and lax.ppermute only.
A program may use at most 128 MiB of HBM per device.

```python
import math
import jax
import jax.numpy as jnp
import numpy as np
from jax import lax

D = 2048
F = 768
RDEV = 448
BLK = 128
EXPERTS = 64
ROWS = 28672
CAP = 14
SLOTS = 896
MAXB = 7
N_EP = 64


def draw_blocks(key, part):
    first, second, third = jax.random.split(jax.random.fold_in(key, 7), 3)
    values = jax.random.randint(first, (2, N_EP), 1, MAXB + 1)
    highest = jax.random.randint(second, (2,), 0, N_EP)
    lowest = jax.random.randint(third, (2,), 0, N_EP)
    columns = jnp.arange(N_EP, dtype=jnp.int32)
    values = jnp.where(columns[None, :] == lowest[:, None], 1, values)
    values = jnp.where(columns[None, :] == highest[:, None], MAXB, values)
    return values.astype(jnp.int32)


def place_ends(drawn, stream_key, smallest, top_value):
    index_at = [jax.random.randint(jax.random.fold_in(stream_key, axis), (), 0, length) for axis, length in enumerate(drawn.shape)]
    main_axis = drawn.shape.index(max(drawn.shape))
    neighbour = index_at[:main_axis] + [(index_at[main_axis] + 1) % drawn.shape[main_axis]] + index_at[main_axis + 1:]
    return drawn.at[tuple(index_at)].set(smallest).at[tuple(neighbour)].set(top_value)


def steps_of(own_key, shape, cuts, least, largest):
    level, own = 1.0, jax.random.fold_in(own_key, 6)
    for axis_at, parts in cuts:
        draws = jnp.exp(jax.random.uniform(jax.random.fold_in(own, axis_at), (parts,), jnp.float32, least / len(cuts), largest / len(cuts)))
        level = level * jnp.repeat(draws, shape[axis_at] // parts).reshape([-1 if axis == axis_at else 1 for axis in range(len(shape))])
    return level


def rank_bounds(number_of, skew):
    portions = [(1 << 20) // math.isqrt(grade ** skew) + 1 for grade in range(1, number_of + 1)]
    scale = 1 + sum(portions) // (1 << 30)
    return np.cumsum(np.array([max(1, weight // scale) for weight in portions]))


def ranked_ids(own_key, dims, number_of, lean):
    grid = rank_bounds(number_of, lean)
    ticket = jax.random.randint(jax.random.fold_in(own_key, 1), dims, 0, int(grid[number_of - 1]))
    rank = jnp.searchsorted(jnp.asarray(grid, jnp.int32), ticket, side="right")
    return jax.random.permutation(jax.random.fold_in(own_key, 2), number_of)[rank].astype(jnp.int32)


def assign_block(key, own, number, rows, number_of, top, most, skew):
    order = jax.random.permutation(key, number_of)
    heavy_load, common = shares(number_of, rows * top, most, skew, True), shares(number_of, rows * top, most, skew, False)
    places = jnp.arange(number_of)

    def named(sizes, rotation):
        used = int((sizes > 0).sum())
        fixed = max(1, used // 4)
        moved = fixed + (places - fixed + rotation * (used - fixed)) % max(1, number_of - fixed)
        return jnp.zeros((number_of,), jnp.int32).at[order[jnp.where(places < fixed, places, moved)]].set(jnp.asarray(sizes, jnp.int32))

    sizes = jnp.where(number % 4 == 0, named(heavy_load, number // 4), named(common, number - number // 4 - 1))
    mixed = jax.random.permutation(jax.random.fold_in(own, 3), number_of)
    giver, taker = mixed[0:number_of // 2 * 2:2], mixed[1:number_of // 2 * 2:2]
    slack = jnp.minimum(sizes[giver] - 1, most - sizes[taker]) // 2
    slack = jnp.where((giver == order[0]) | (taker == order[0]) | (sizes[taker] == 0), 0, jnp.maximum(slack, 0))
    moved = jax.random.randint(jax.random.fold_in(own, 4), (number_of // 2,), 0, 1 << 20) % (slack + 1)
    sizes = sizes.at[giver].add(-moved).at[taker].add(moved)
    items = jnp.searchsorted(jnp.cumsum(sizes), jnp.arange(rows * top), side="right").astype(jnp.int32)
    listing = items.reshape(top, rows).T
    listing = listing[jax.random.permutation(jax.random.fold_in(own, 1), rows)]
    rotation = jax.random.randint(jax.random.fold_in(own, 2), (rows, 1), 0, top)
    return jnp.take_along_axis(listing, (jnp.arange(top)[None, :] + rotation) % top, axis=1)


def shares(count, total, most, skew, full):
    loads = [(1 << 20) // math.isqrt(rank ** skew) + 1 for rank in range(1, count + 1)]
    largest = most if full else min(most, max(-(-total // count), total * loads[0] // sum(loads)))
    least = 1 if total - largest >= count - 1 else 0
    counts, rest = [largest] + [least] * (count - 1), total - largest - least * (count - 1)
    while rest > 0:
        movable = [i for i in range(1, count) if counts[i] < largest] or [i for i in range(1, count) if counts[i] < most]
        whole, left = sum([loads[i] for i in movable]), rest
        for i in movable:
            extra = min(most - counts[i], max(1, left * loads[i] // whole), rest)
            counts[i] = counts[i] + extra
            rest = rest - extra
    return np.array(counts)


def bell_draw(stream_key, extent, scale, most, shards=(), held_as=jnp.bfloat16):
    values = scale * jax.random.normal(stream_key, extent, jnp.float32)
    if shards:
        values = values * steps_of(stream_key, extent, shards, -0.22, 0.18)
    return jnp.clip(values, -most, most).astype(held_as)


def setup_inputs(seed: int = 0) -> dict:
    key_of = jax.random.split(jax.random.key(seed), 8)
    activations = bell_draw(key_of[0], (2, ROWS, D), 1.0, 6.0, ((0, 2), (1, 64)))
    routes_keys = jax.random.split(jax.random.fold_in(key_of[1], 1), 2 * ROWS // RDEV)
    routes_turns = jax.random.permutation(jax.random.fold_in(key_of[1], 3), 2 * ROWS // RDEV)
    routes = jax.vmap(lambda own, number: assign_block(jax.random.fold_in(key_of[1], 2), own, number, RDEV, N_EP, 1, CAP, 2))(routes_keys, routes_turns).reshape((2, ROWS, 1))
    blocks = draw_blocks(jax.random.fold_in(key_of[7], 71), 0)
    row_scale = bell_draw(key_of[3], (2, ROWS), 1.0, 4.0, ((0, 2), (1, 64)))
    gate_up = bell_draw(key_of[4], (EXPERTS, D, 2 * F), D ** -0.5, 0.125, ((0, 64),))
    down_weight = bell_draw(key_of[5], (EXPERTS, F, D), F ** -0.5, 0.21875, ((0, 64),))
    slot_map = place_ends(ranked_ids(key_of[6], (EXPERTS,), EXPERTS, 2), jax.random.fold_in(key_of[6], 3), 0, EXPERTS - 1).astype(jnp.int32)
    return dict(activations=activations, routes=routes, blocks=blocks, row_scale=row_scale, gate_up=gate_up, down_weight=down_weight, slot_map=slot_map)


def silu_slope(value):
    sigma = jax.nn.sigmoid(value)
    return sigma * (1.0 + value * (1.0 - sigma))

def train_expert(inputs, scales, gate_up, down_weight):
    width = gate_up.shape[1] // 2
    projected = jnp.dot(inputs, gate_up, preferred_element_type=jnp.float32)
    gate = projected[:, :width]
    upward = projected[:, width:]
    hidden = (jax.nn.silu(gate) * upward).astype(jnp.bfloat16)
    output = jnp.dot(hidden, down_weight, preferred_element_type=jnp.float32)
    out_grad = (scales.astype(jnp.float32)[:, None] * output).astype(jnp.bfloat16)
    down_grad = lax.dot_general(hidden, out_grad, (((0,), (0,)), ((), ())), preferred_element_type=jnp.float32)
    hidden_grad = lax.dot_general(out_grad, down_weight, (((1,), (1,)), ((), ())), preferred_element_type=jnp.float32)
    both_grad = jnp.concatenate([hidden_grad * upward * silu_slope(gate), hidden_grad * jax.nn.silu(gate)], axis=1).astype(jnp.bfloat16)
    gate_grad = lax.dot_general(inputs, both_grad, (((0,), (0,)), ((), ())), preferred_element_type=jnp.float32)
    input_grad = lax.dot_general(both_grad, gate_up, (((1,), (1,)), ((), ())), preferred_element_type=jnp.float32).astype(jnp.bfloat16)
    step_size = 0.03 / math.sqrt(RDEV)
    new_gate = (gate_up.astype(jnp.float32) - step_size * gate_grad).astype(jnp.bfloat16)
    new_down = (down_weight.astype(jnp.float32) - step_size * down_grad).astype(jnp.bfloat16)
    return (input_grad, new_gate, new_down)

def serve_expert(inputs, scales, gate_up, down_weight):
    width = gate_up.shape[1] // 2
    projected = jnp.dot(inputs, gate_up, preferred_element_type=jnp.float32)
    hidden = (jax.nn.silu(projected[:, :width]) * projected[:, width:]).astype(jnp.bfloat16)
    output = jnp.dot(hidden, down_weight, preferred_element_type=jnp.float32)
    return (scales.astype(jnp.float32)[:, None] * output).astype(jnp.bfloat16)

def slot_table(target, limits):
    labels = jnp.arange(N_EP, dtype=jnp.int32)
    onehot = (target[:, None] == labels[None, :]).astype(jnp.int32)
    before = jnp.cumsum(onehot, axis=0) - onehot
    order = lax.optimization_barrier(jnp.sum(before * onehot, axis=1))
    bound = lax.optimization_barrier(jnp.sum(onehot * limits[None, :], axis=1))
    places = jnp.where(order < bound, target * SLOTS + order, N_EP * SLOTS).astype(jnp.int32)
    table = jnp.full((N_EP * SLOTS + 1,), ROWS, jnp.int32).at[places].set(jnp.arange(ROWS, dtype=jnp.int32))
    return table[:N_EP * SLOTS].reshape(N_EP, SLOTS)

def reference(activations, routes, blocks, row_scale, gate_up, down_weight, slot_map):
    zero_row = jnp.zeros((1, D), activations.dtype)
    zero_scale = jnp.zeros((1,), row_scale.dtype)
    train_table = slot_table(routes[0, :, 0], blocks[0] * BLK)
    serve_table = slot_table(routes[1, :, 0], blocks[1] * BLK)
    train_rows = jnp.concatenate([activations[0], zero_row], axis=0)
    train_scale = jnp.concatenate([row_scale[0], zero_scale], axis=0)
    serve_rows = jnp.concatenate([activations[1], zero_row], axis=0)
    serve_scale = jnp.concatenate([row_scale[1], zero_scale], axis=0)

    def train_one(items):
        table, gate_part, down_part = items
        return train_expert(train_rows[table], train_scale[table], gate_part, down_part)
    grads, new_gate, new_down = lax.map(train_one, (train_table, gate_up, down_weight))
    train_out = jnp.zeros((ROWS + 1, D), grads.dtype).at[train_table.reshape(-1)].set(grads.reshape(-1, D))[:ROWS]

    def serve_one(items):
        table, expert = items
        gate_part = lax.dynamic_index_in_dim(new_gate, expert, 0, keepdims=False)
        down_part = lax.dynamic_index_in_dim(new_down, expert, 0, keepdims=False)
        return serve_expert(serve_rows[table], serve_scale[table], gate_part, down_part)
    served = lax.map(serve_one, (serve_table, slot_map))
    serve_out = jnp.zeros((ROWS + 1, D), served.dtype).at[serve_table.reshape(-1)].set(served.reshape(-1, D))[:ROWS]
    return jnp.stack([train_out, serve_out])
```

```python
import math

import jax
import jax.numpy as jnp
from jax import lax
from jax.experimental import pallas as pl
from jax.experimental.pallas import tpu as pltpu
from jax.sharding import PartitionSpec as P

BLK = 128
PART = 7
BOX = 8
COUNT = 8
LANES = 128
SWAP = [(0, 1), (1, 0)]
F32 = jnp.float32
BF16 = jnp.bfloat16
NT = (((1,), (1,)), ((), ()))


def params(mib=56):
    return pltpu.CompilerParams(vmem_limit_bytes=mib << 20)


def iota(shape, dim):
    return lax.broadcasted_iota(jnp.int32, shape, dim)


def anywhere():
    return pl.BlockSpec(memory_space=pl.ANY)


def vmem():
    return pl.BlockSpec(memory_space=pltpu.VMEM)


def smem():
    return pl.BlockSpec(memory_space=pltpu.SMEM)


def order_of(target, members):
    rows = target.shape[1]
    named = iota((members, rows), 0) == target
    onehot = named.astype(BF16)
    upper = (iota((rows, rows), 0) < iota((rows, rows), 1)).astype(BF16)
    before = jnp.dot(onehot, upper, preferred_element_type=F32)
    return jnp.sum(jnp.where(named, before, 0.0), axis=0, keepdims=True).astype(jnp.int32)


def pack_kernel(group, members, scal, tok_a, tok_b, route_a, route_b, scale_a, scale_b, out, tok, sem):
    half = scal[0]
    own = half == group

    @pl.when(own)
    def _():
        pltpu.make_async_copy(tok_a, tok, sem).start()

    @pl.when(jnp.logical_not(own))
    def _():
        pltpu.make_async_copy(tok_b, tok, sem).start()

    target = jnp.where(own, route_a[...], route_b[...])
    scale = jnp.where(own, scale_a[...].astype(F32), scale_b[...].astype(F32))
    rows = target.shape[1]
    slots = members * BOX
    order = order_of(target, members) - PART * half
    inside = (order >= 0) & (order < PART)
    place = jnp.where(inside, target * BOX + order, -1)
    placer = (iota((slots, rows), 0) == place).astype(BF16)
    tags = (iota((slots, rows), 0) == target * BOX + PART).astype(BF16)
    lane = iota((LANES, rows), 0)
    told = jnp.where((lane == order) & inside, scale, jnp.where(lane == COUNT, 1.0, 0.0)).astype(BF16)
    info = lax.dot_general(tags, told, NT, preferred_element_type=F32)
    pltpu.make_async_copy(tok_a, tok, sem).wait()
    first = jnp.dot(placer, tok[:, :LANES], preferred_element_type=F32) + info
    out[:, :LANES] = first.astype(BF16)
    rest = tok.shape[1] - LANES
    out[:, LANES:] = jnp.dot(placer, tok[:, LANES:], preferred_element_type=F32).astype(BF16)


def pack(group, members, scal, tok_a, tok_b, route_a, route_b, scale_a, scale_b):
    slots = members * BOX
    width = tok_a.shape[1]
    return pl.pallas_call(
        lambda *refs: pack_kernel(group, members, *refs),
        out_shape=jax.ShapeDtypeStruct((slots, width), BF16),
        in_specs=[smem(), anywhere(), anywhere(), vmem(), vmem(), vmem(), vmem()],
        out_specs=vmem(),
        scratch_shapes=[pltpu.VMEM(tok_a.shape, BF16), pltpu.SemaphoreType.DMA],
        compiler_params=params(),
        name=f"pack{group}",
    )(scal, tok_a, tok_b, route_a, route_b, scale_a, scale_b)


def kept_and_scale(head, half, limit):
    slots = head.shape[0]
    row = iota((slots, slots), 0) // BOX
    col = iota((slots, slots), 1)
    tag = (col % BOX) == PART
    mine = (tag & (col // BOX == row)).astype(BF16)
    lower = (tag & (col // BOX < row)).astype(BF16)
    here = jnp.dot(mine, head, preferred_element_type=F32)
    below = jnp.dot(lower, head, preferred_element_type=F32)
    lane = iota((slots, LANES), 1)
    place = iota((slots, LANES), 0) % BOX
    scale = jnp.sum(jnp.where(lane == place, here, 0.0), axis=1, keepdims=True)
    total = jnp.sum(jnp.where(lane == COUNT, here, 0.0), axis=1, keepdims=True)
    ahead = jnp.sum(jnp.where(lane == COUNT, below, 0.0), axis=1, keepdims=True)
    k = iota((slots, 1), 0) % BOX
    index = (k + PART * half).astype(F32)
    kept = (k < PART) & (index < total) & (ahead + index < limit.astype(F32))
    return kept, scale


def limit_of(group, scal, blocks_a, blocks_b):
    own = scal[0] == group
    at = scal[1]
    return jnp.where(own, blocks_a[0, at], blocks_b[0, at]) * BLK


def train_kernel(scal, blocks_a, blocks_b, x_h, gu_h, dw_h, dg_own, dg_send, gg_own, gg_send, bg_h,
                 x, gu, dw, gate, up, hid, og, bg, hid_t, x_t, dg, gg, sem):
    half = scal[0]
    d, f2 = gu.shape
    f = f2 // 2
    fc, dc = 256, 512
    nf, nd = f // fc, d // dc

    def load_gu(i, which):
        cols = pl.ds(pl.multiple_of(which * f + i * fc, fc), fc)
        return pltpu.make_async_copy(gu_h.at[:, cols], gu.at[:, cols], sem.at[2 + 2 * i + which])

    load_x = pltpu.make_async_copy(x_h, x, sem.at[0])
    load_dw = pltpu.make_async_copy(dw_h, dw, sem.at[1])
    load_x.start()
    for i in range(nf):
        load_gu(i, 0).start()
        load_gu(i, 1).start()
    load_dw.start()
    load_x.wait()
    kept, scale = kept_and_scale(x[:, :LANES], half, limit_of(0, scal, blocks_a, blocks_b))
    keep = jnp.where(kept, 1.0, 0.0)

    def mask(c, _):
        cols = pl.ds(pl.multiple_of(c * fc, fc), fc)
        clean = (x[:, cols].astype(F32) * keep).astype(BF16)
        x[:, cols] = clean
        x_t[cols, :] = clean.T
        return 0

    lax.fori_loop(0, d // fc, mask, 0)

    def project(i, _):
        load_gu(i, 0).wait()
        load_gu(i, 1).wait()
        left = pl.ds(pl.multiple_of(i * fc, fc), fc)
        right = pl.ds(pl.multiple_of(f + i * fc, fc), fc)
        g = jnp.dot(x[...], gu[:, left], preferred_element_type=F32)
        u = jnp.dot(x[...], gu[:, right], preferred_element_type=F32)
        h = (g * jax.nn.sigmoid(g) * u).astype(BF16)
        gate[:, left] = g
        up[:, left] = u
        hid[:, left] = h
        hid_t[left, :] = h.T
        return 0

    lax.fori_loop(0, nf, project, 0)
    load_dw.wait()

    def outputs(c, _):
        cols = pl.ds(pl.multiple_of(c * dc, dc), dc)
        o = jnp.dot(hid[...], dw[:, cols], preferred_element_type=F32)
        og[:, cols] = (scale * o).astype(BF16)
        return 0

    lax.fori_loop(0, nd, outputs, 0)

    def down_part(c, _):
        cols = pl.ds(pl.multiple_of(c * dc, dc), dc)
        dg[:, cols] = jnp.dot(hid_t[...], og[:, cols], preferred_element_type=F32).astype(BF16)
        return 0

    lax.fori_loop(0, nd, down_part, 0)

    def store(src, own, send, lo, size, s):
        def copies(b):
            part = src.at[pl.ds(b * size, size)]
            return pltpu.make_async_copy(part, (own, send)[b != lo], sem.at[s + b])

        return copies

    for h in range(2):
        @pl.when(half == h)
        def _():
            for b in range(2):
                store(dg, dg_own, dg_send, h, f // 2, 2 + 2 * nf)(b).start()

    def hidden_back(i, _):
        left = pl.ds(pl.multiple_of(i * fc, fc), fc)
        right = pl.ds(pl.multiple_of(f + i * fc, fc), fc)
        hg = lax.dot_general(og[...], dw[left, :], NT, preferred_element_type=F32)
        g = gate[:, left]
        s = jax.nn.sigmoid(g)
        bg[:, left] = (hg * up[:, left] * (s * (1.0 + g * (1.0 - s)))).astype(BF16)
        bg[:, right] = (hg * (g * s)).astype(BF16)
        return 0

    lax.fori_loop(0, nf, hidden_back, 0)
    out_bg = pltpu.make_async_copy(bg, bg_h, sem.at[6 + 2 * nf])
    out_bg.start()
    for b in range(2):
        rows = pl.ds(b * (d // 2), d // 2)

        def gate_part(c, _):
            cols = pl.ds(pl.multiple_of(c * fc, fc), fc)
            gg[rows, cols] = jnp.dot(x_t[rows, :], bg[:, cols], preferred_element_type=F32).astype(BF16)
            return 0

        lax.fori_loop(0, f2 // fc, gate_part, 0)
        for h in range(2):
            @pl.when(half == h)
            def _():
                store(gg, gg_own, gg_send, h, d // 2, 4 + 2 * nf)(b).start()
    for b in range(2):
        store(dg, dg_own, dg_send, 0, f // 2, 2 + 2 * nf)(b).wait()
        store(gg, gg_own, gg_send, 0, d // 2, 4 + 2 * nf)(b).wait()
    out_bg.wait()


def train(scal, blocks_a, blocks_b, x, gate_up, down):
    slots, d = x.shape
    f2 = gate_up.shape[1]
    f = f2 // 2
    dg = jax.ShapeDtypeStruct((f // 2, d), BF16)
    gg = jax.ShapeDtypeStruct((d // 2, f2), BF16)
    nf = f // 256
    return pl.pallas_call(
        train_kernel,
        out_shape=(dg, dg, gg, gg, jax.ShapeDtypeStruct((slots, f2), BF16)),
        in_specs=[smem(), smem(), smem(), anywhere(), anywhere(), anywhere()],
        out_specs=(anywhere(),) * 5,
        scratch_shapes=[
            pltpu.VMEM((slots, d), BF16), pltpu.VMEM((d, f2), BF16), pltpu.VMEM((f, d), BF16),
            pltpu.VMEM((slots, f), F32), pltpu.VMEM((slots, f), F32), pltpu.VMEM((slots, f), BF16),
            pltpu.VMEM((slots, d), BF16), pltpu.VMEM((slots, f2), BF16), pltpu.VMEM((f, slots), BF16),
            pltpu.VMEM((d, slots), BF16), pltpu.VMEM((f, d), BF16), pltpu.VMEM((d, f2), BF16),
            pltpu.SemaphoreType.DMA((7 + 2 * nf,)),
        ],
        compiler_params=params(),
        name="train",
    )(scal, blocks_a, blocks_b, x, gate_up, down)


def update_down_kernel(eta, scal, a, b, w, out):
    new = w[...].astype(F32) - eta * (a[...].astype(F32) + b[...].astype(F32))
    high, wide = out.shape[2:]
    for i in range(out.shape[0]):
        for j in range(out.shape[1]):
            out[i, j] = new[i * high:(i + 1) * high, j * wide:(j + 1) * wide].astype(BF16)


def update_down(eta, scal, a, b, w):
    rows, d = a.shape
    high, wide, steps = rows // 8, d // 8, 4
    tall = rows // steps
    mine = pl.BlockSpec((tall, d), lambda i, s: (i, 0))
    return pl.pallas_call(
        lambda *refs: update_down_kernel(eta, *refs),
        out_shape=jax.ShapeDtypeStruct((8, 8, high, wide), BF16),
        grid_spec=pltpu.PrefetchScalarGridSpec(
            num_scalar_prefetch=1,
            grid=(steps,),
            in_specs=[mine, mine, pl.BlockSpec((tall, d), lambda i, s: (s[0] * steps + i, 0))],
            out_specs=pl.BlockSpec((8 // steps, 8, high, wide), lambda i, s: (i, 0, 0, 0)),
        ),
        compiler_params=params(),
        name="update_down",
    )(scal, a, b, w)


def update_gate_kernel(eta, scal, a, b, w, out):
    out[...] = (w[...].astype(F32) - eta * (a[...].astype(F32) + b[...].astype(F32))).astype(BF16)


def update_gate(eta, scal, a, b, w):
    rows, f2 = a.shape
    steps = 4
    tall = rows // steps
    mine = pl.BlockSpec((tall, f2), lambda i, s: (i, 0))
    return pl.pallas_call(
        lambda *refs: update_gate_kernel(eta, *refs),
        out_shape=jax.ShapeDtypeStruct((rows, f2), BF16),
        grid_spec=pltpu.PrefetchScalarGridSpec(
            num_scalar_prefetch=1,
            grid=(steps,),
            in_specs=[mine, mine, pl.BlockSpec((tall, f2), lambda i, s: (s[0] * steps + i, 0))],
            out_specs=mine,
        ),
        compiler_params=params(),
        name="update_gate",
    )(scal, a, b, w)


def choose_kernel(slot_map, src, out, sem):
    count = out.shape[0]

    def copy(i):
        return pltpu.make_async_copy(src.at[slot_map[i]], out.at[i], sem.at[i])

    def start(i, _):
        copy(i).start()
        return 0

    def wait(i, _):
        copy(i).wait()
        return 0

    lax.fori_loop(0, count, start, 0)
    lax.fori_loop(0, count, wait, 0)


def choose(name, slot_map, pieces):
    return pl.pallas_call(
        choose_kernel,
        out_shape=jax.ShapeDtypeStruct(pieces.shape, BF16),
        in_specs=[smem(), anywhere()],
        out_specs=anywhere(),
        scratch_shapes=[pltpu.SemaphoreType.DMA((pieces.shape[0],))],
        compiler_params=params(4),
        name=name,
    )(slot_map, pieces)


def serve_kernel(scal, blocks_a, blocks_b, x_h, gu_a, gu_b, dw_a, dw_b, out, x, gu, dw, hid, sem):
    half = scal[0]
    d, f2 = gu.shape
    f = f2 // 2
    fc, dc = 256, 512

    load_x = pltpu.make_async_copy(x_h, x, sem.at[0])

    def load_gu(src, place, s):
        rows = pl.ds(pl.multiple_of(place * (d // 2), d // 2), d // 2)
        return pltpu.make_async_copy(src, gu.at[rows], sem.at[s])

    def load_dw(src, place, j, s):
        wide = d // 8
        return pltpu.make_async_copy(src.at[:, j], dw.at[place, :, :, pl.ds(j * wide, wide)], sem.at[s + j])

    load_x.start()
    load_gu(gu_a, half, 1).start()
    load_gu(gu_b, 1 - half, 2).start()
    for j in range(8):
        load_dw(dw_a, half, j, 3).start()
        load_dw(dw_b, 1 - half, j, 11).start()
    load_x.wait()
    kept, scale = kept_and_scale(x[:, :LANES], half, limit_of(1, scal, blocks_a, blocks_b))
    load_gu(gu_a, half, 1).wait()
    load_gu(gu_b, 1 - half, 2).wait()

    def project(i, _):
        left = pl.ds(pl.multiple_of(i * fc, fc), fc)
        right = pl.ds(pl.multiple_of(f + i * fc, fc), fc)
        g = jnp.dot(x[...], gu[:, left], preferred_element_type=F32)
        u = jnp.dot(x[...], gu[:, right], preferred_element_type=F32)
        hid[:, left] = (g * jax.nn.sigmoid(g) * u).astype(BF16)
        return 0

    lax.fori_loop(0, f // fc, project, 0)
    for j in range(8):
        load_dw(dw_a, half, j, 3).wait()
        load_dw(dw_b, 1 - half, j, 11).wait()

    def outputs(c, _):
        cols = pl.ds(pl.multiple_of(c * dc, dc), dc)
        o = jnp.dot(hid[...], dw[:, :, :, cols].reshape(f, dc), preferred_element_type=F32)
        out[:, cols] = jnp.where(kept, scale * o, 0.0).astype(BF16)
        return 0

    lax.fori_loop(0, d // dc, outputs, 0)


def serve(scal, blocks_a, blocks_b, x, gu_a, gu_b, dw_a, dw_b):
    slots, d = x.shape
    f2 = gu_a.shape[1]
    high = dw_a.shape[2]
    return pl.pallas_call(
        serve_kernel,
        out_shape=jax.ShapeDtypeStruct((slots, d), BF16),
        in_specs=[smem(), smem(), smem()] + [anywhere()] * 5,
        out_specs=vmem(),
        scratch_shapes=[
            pltpu.VMEM((slots, d), BF16), pltpu.VMEM((d, f2), BF16), pltpu.VMEM((2, 8, high, d), BF16),
            pltpu.VMEM((slots, f2 // 2), BF16), pltpu.SemaphoreType.DMA((19,)),
        ],
        compiler_params=params(),
        name="serve",
    )(scal, blocks_a, blocks_b, x, gu_a, gu_b, dw_a, dw_b)


def unpack_kernel(members, scal, route, t_own, t_recv, p_own, p_recv, out, low, high, sem):
    half = scal[0]

    @pl.when(half == 0)
    def _():
        pltpu.make_async_copy(t_own, low, sem.at[0]).start()
        pltpu.make_async_copy(t_recv, high, sem.at[1]).start()

    @pl.when(half == 1)
    def _():
        pltpu.make_async_copy(p_recv, low, sem.at[0]).start()
        pltpu.make_async_copy(p_own, high, sem.at[1]).start()

    target = route[...]
    rows = target.shape[1]
    order = order_of(target, members)
    eye = (iota((rows, rows), 0) == iota((rows, rows), 1)).astype(BF16)
    pair = jnp.where(iota((BOX, rows), 0) == 0, target, order).astype(F32).astype(BF16)
    column = lax.dot_general(eye, pair, NT, preferred_element_type=F32).astype(jnp.int32)
    goal, rank = column[:, 0:1], column[:, 1:2]
    slots = members * BOX
    at = iota((rows, slots), 1)
    pick_low = (at == jnp.where(rank < PART, goal * BOX + rank, -1)).astype(BF16)
    pick_high = (at == jnp.where(rank >= PART, goal * BOX + rank - PART, -1)).astype(BF16)
    pltpu.make_async_copy(t_own, low, sem.at[0]).wait()
    pltpu.make_async_copy(t_own, high, sem.at[1]).wait()
    total = jnp.dot(pick_low, low[...], preferred_element_type=F32)
    total = total + jnp.dot(pick_high, high[...], preferred_element_type=F32)
    out[...] = total.astype(BF16)


def unpack(members, scal, route, t_own, t_recv, p_own, p_recv):
    slots, d = t_own.shape
    rows = route.shape[1]
    return pl.pallas_call(
        lambda *refs: unpack_kernel(members, *refs),
        out_shape=jax.ShapeDtypeStruct((rows, d), BF16),
        in_specs=[smem(), vmem()] + [anywhere()] * 4,
        out_specs=vmem(),
        scratch_shapes=[pltpu.VMEM((slots, d), BF16), pltpu.VMEM((slots, d), BF16), pltpu.SemaphoreType.DMA((2,))],
        compiler_params=params(),
        name="unpack",
    )(scal, route, t_own, t_recv, p_own, p_recv)


def swap(value):
    return lax.ppermute(value, "half", SWAP)


def spread(value):
    members = lax.axis_size("ep")
    shape = value.shape
    boxes = value.reshape((members, -1) + shape[-1:])
    return lax.all_to_all(boxes, "ep", split_axis=0, concat_axis=0, tiled=True).reshape(shape)


def shards(activations, routes, blocks, row_scale, gate_up, down_weight, slot_map):
    members = lax.axis_size("ep")
    tokens = activations[0]
    row_count = tokens.shape[0]
    route = routes.reshape(1, row_count)
    gate_up, down_weight = gate_up[0], down_weight[0]
    scal = jnp.stack([lax.axis_index("half"), lax.axis_index("ep")]).astype(jnp.int32)
    eta = 0.03 / math.sqrt(row_count)

    tokens_b, route_b, scale_b, blocks_b = swap(tokens), swap(route), swap(row_scale), swap(blocks)
    parts = (scal, tokens, tokens_b, route, route_b, row_scale, scale_b)
    train_rows = spread(pack(0, members, *parts))
    serve_rows = spread(pack(1, members, *parts))

    down_own, down_send, gate_own, gate_send, both_grad = train(
        scal, blocks, blocks_b, train_rows, gate_up, down_weight
    )
    new_down = update_down(eta, scal, down_own, swap(down_send), down_weight)
    high, wide = new_down.shape[2:]
    down_pieces = spread(new_down.reshape(members * high, wide)).reshape(members, high, wide)
    new_gate = update_gate(eta, scal, gate_own, swap(gate_send), gate_up)
    gate_pieces = spread(new_gate).reshape(members, -1, new_gate.shape[1])
    both_grad, _ = lax.optimization_barrier((both_grad, new_gate))
    input_grad = lax.dot_general(both_grad, gate_up, NT, preferred_element_type=F32).astype(BF16)
    train_back = spread(input_grad)
    train_other = swap(train_back)

    slot_down = spread(choose("choose_down", slot_map, down_pieces).reshape(members * high, wide))
    slot_down = slot_down.reshape(new_down.shape)
    down_other = swap(slot_down)
    slot_gate = spread(choose("choose_gate", slot_map, gate_pieces).reshape(new_gate.shape))
    gate_other = swap(slot_gate)
    served = serve(scal, blocks, blocks_b, serve_rows, slot_gate, gate_other, slot_down, down_other)
    serve_back = spread(served)
    serve_other = swap(serve_back)
    return unpack(members, scal, route, train_back, train_other, serve_back, serve_other)[None]


def solution(mesh):
    placed = (
        P("half", "ep", None),
        P("half", "ep", None),
        P("half", None),
        P("half", "ep"),
        P("ep", None, None),
        P("ep", None, None),
        P(),
    )
    return jax.shard_map(
        shards, mesh=mesh, in_specs=placed, out_specs=P("half", "ep", None), check_vma=False
    )
```

```python
import math

import jax
import jax.numpy as jnp
from jax import lax
from jax.experimental import pallas as pl
from jax.experimental.pallas import tpu as pltpu
from jax.sharding import PartitionSpec as P


BLK = 128
PART = 7
BOX = 8
COUNT = 8
LANES = 128
SWAP = [(0, 1), (1, 0)]
F32 = jnp.float32
BF16 = jnp.bfloat16
NT = (((1,), (1,)), ((), ()))


def params(mib=56):
    return pltpu.CompilerParams(vmem_limit_bytes=mib << 20)


def iota(shape, dim):
    return lax.broadcasted_iota(jnp.int32, shape, dim)


def anywhere():
    return pl.BlockSpec(memory_space=pl.ANY)


def vmem():
    return pl.BlockSpec(memory_space=pltpu.VMEM)


def smem():
    return pl.BlockSpec(memory_space=pltpu.SMEM)


def order_of(target, members):
    rows = target.shape[1]
    named = iota((members, rows), 0) == target
    onehot = named.astype(BF16)
    upper = (iota((rows, rows), 0) < iota((rows, rows), 1)).astype(BF16)
    before = jnp.dot(onehot, upper, preferred_element_type=F32)
    return jnp.sum(jnp.where(named, before, 0.0), axis=0, keepdims=True).astype(jnp.int32)


def pack_kernel(group, members, scal, tok_a, tok_b, route_a, route_b, scale_a, scale_b, out, tok, sem):
    half = scal[0]
    own = half == group

    @pl.when(own)
    def _():
        pltpu.make_async_copy(tok_a, tok, sem).start()

    @pl.when(jnp.logical_not(own))
    def _():
        pltpu.make_async_copy(tok_b, tok, sem).start()

    target = jnp.where(own, route_a[...], route_b[...])
    scale = jnp.where(own, scale_a[...].astype(F32), scale_b[...].astype(F32))
    rows = target.shape[1]
    slots = members * BOX
    order = order_of(target, members) - PART * half
    inside = (order >= 0) & (order < PART)
    place = jnp.where(inside, target * BOX + order, -1)
    placer = (iota((slots, rows), 0) == place).astype(BF16)
    tags = (iota((slots, rows), 0) == target * BOX + PART).astype(BF16)
    lane = iota((LANES, rows), 0)
    told = jnp.where((lane == order) & inside, scale, jnp.where(lane == COUNT, 1.0, 0.0)).astype(BF16)
    info = lax.dot_general(tags, told, NT, preferred_element_type=F32)
    pltpu.make_async_copy(tok_a, tok, sem).wait()
    first = jnp.dot(placer, tok[:, :LANES], preferred_element_type=F32) + info
    out[:, :LANES] = first.astype(BF16)
    out[:, LANES:] = jnp.dot(placer, tok[:, LANES:], preferred_element_type=F32).astype(BF16)


def pack(group, members, scal, tok_a, tok_b, route_a, route_b, scale_a, scale_b):
    slots = members * BOX
    width = tok_a.shape[1]
    return pl.pallas_call(
        lambda *refs: pack_kernel(group, members, *refs),
        out_shape=jax.ShapeDtypeStruct((slots, width), BF16),
        in_specs=[smem(), anywhere(), anywhere(), vmem(), vmem(), vmem(), vmem()],
        out_specs=vmem(),
        scratch_shapes=[pltpu.VMEM(tok_a.shape, BF16), pltpu.SemaphoreType.DMA],
        compiler_params=params(),
    )(scal, tok_a, tok_b, route_a, route_b, scale_a, scale_b)


def kept_and_scale(head, half, limit):
    slots = head.shape[0]
    row = iota((slots, slots), 0) // BOX
    col = iota((slots, slots), 1)
    tag = (col % BOX) == PART
    mine = (tag & (col // BOX == row)).astype(BF16)
    lower = (tag & (col // BOX < row)).astype(BF16)
    here = jnp.dot(mine, head, preferred_element_type=F32)
    below = jnp.dot(lower, head, preferred_element_type=F32)
    lane = iota((slots, LANES), 1)
    place = iota((slots, LANES), 0) % BOX
    scale = jnp.sum(jnp.where(lane == place, here, 0.0), axis=1, keepdims=True)
    total = jnp.sum(jnp.where(lane == COUNT, here, 0.0), axis=1, keepdims=True)
    ahead = jnp.sum(jnp.where(lane == COUNT, below, 0.0), axis=1, keepdims=True)
    k = iota((slots, 1), 0) % BOX
    index = (k + PART * half).astype(F32)
    kept = (k < PART) & (index < total) & (ahead + index < limit.astype(F32))
    return kept, scale


def limit_of(group, scal, blocks_a, blocks_b):
    own = scal[0] == group
    at = scal[1]
    return jnp.where(own, blocks_a[0, at], blocks_b[0, at]) * BLK


def train_kernel(scal, blocks_a, blocks_b, x_h, gu_h, dw_h, hid_h, og_own, og_send, bg_h,
                 x, gu, dw, gate, up, hid, og, bg, sem):
    half = scal[0]
    d, f2 = gu.shape
    f = f2 // 2
    fc, dc = 256, 512
    nf, nd = f // fc, d // dc

    def load_gu(i, which):
        cols = pl.ds(pl.multiple_of(which * f + i * fc, fc), fc)
        return pltpu.make_async_copy(gu_h.at[:, cols], gu.at[:, cols], sem.at[2 + 2 * i + which])

    load_x = pltpu.make_async_copy(x_h, x, sem.at[0])
    load_dw = pltpu.make_async_copy(dw_h, dw, sem.at[1])
    load_x.start()
    for i in range(nf):
        load_gu(i, 0).start()
        load_gu(i, 1).start()
    load_dw.start()
    load_x.wait()
    kept, scale = kept_and_scale(x[:, :LANES], half, limit_of(0, scal, blocks_a, blocks_b))
    keep = jnp.where(kept, 1.0, 0.0)

    def project(i, _):
        load_gu(i, 0).wait()
        load_gu(i, 1).wait()
        left = pl.ds(pl.multiple_of(i * fc, fc), fc)
        right = pl.ds(pl.multiple_of(f + i * fc, fc), fc)
        g = jnp.dot(x[...], gu[:, left], preferred_element_type=F32)
        u = jnp.dot(x[...], gu[:, right], preferred_element_type=F32)
        gate[:, left] = g
        up[:, left] = u
        hid[:, left] = (keep * (g * jax.nn.sigmoid(g) * u)).astype(BF16)
        return 0

    lax.fori_loop(0, nf, project, 0)
    out_hid = pltpu.make_async_copy(hid, hid_h, sem.at[2 + 2 * nf])
    out_hid.start()
    load_dw.wait()

    def outputs(c, _):
        cols = pl.ds(pl.multiple_of(c * dc, dc), dc)
        o = jnp.dot(hid[...], dw[:, cols], preferred_element_type=F32)
        og[:, cols] = (scale * o).astype(BF16)
        return 0

    lax.fori_loop(0, nd, outputs, 0)

    def out_og(which, place):
        cols = pl.ds(pl.multiple_of(place * (d // 2), d // 2), d // 2)
        return pltpu.make_async_copy(og.at[:, cols], (og_own, og_send)[which], sem.at[3 + 2 * nf + which])

    out_og(0, half).start()
    out_og(1, 1 - half).start()

    def hidden_back(i, _):
        left = pl.ds(pl.multiple_of(i * fc, fc), fc)
        right = pl.ds(pl.multiple_of(f + i * fc, fc), fc)
        hg = lax.dot_general(og[...], dw[left, :], NT, preferred_element_type=F32)
        g = gate[:, left]
        s = jax.nn.sigmoid(g)
        bg[:, left] = (hg * up[:, left] * (s * (1.0 + g * (1.0 - s)))).astype(BF16)
        bg[:, right] = (hg * (g * s)).astype(BF16)
        return 0

    lax.fori_loop(0, nf, hidden_back, 0)
    out_bg = pltpu.make_async_copy(bg, bg_h, sem.at[5 + 2 * nf])
    out_bg.start()
    out_hid.wait()
    out_og(0, half).wait()
    out_og(1, 1 - half).wait()
    out_bg.wait()


def train(scal, blocks_a, blocks_b, x, gate_up, down):
    slots, d = x.shape
    f2 = gate_up.shape[1]
    f = f2 // 2
    half_rows = jax.ShapeDtypeStruct((slots, d // 2), BF16)
    return pl.pallas_call(
        train_kernel,
        out_shape=(
            jax.ShapeDtypeStruct((slots, f), BF16), half_rows, half_rows, jax.ShapeDtypeStruct((slots, f2), BF16)
        ),
        in_specs=[smem(), smem(), smem(), anywhere(), anywhere(), anywhere()],
        out_specs=(anywhere(),) * 4,
        scratch_shapes=[
            pltpu.VMEM((slots, d), BF16), pltpu.VMEM((d, f2), BF16), pltpu.VMEM((f, d), BF16),
            pltpu.VMEM((slots, f), F32), pltpu.VMEM((slots, f), F32), pltpu.VMEM((slots, f), BF16),
            pltpu.VMEM((slots, d), BF16), pltpu.VMEM((slots, f2), BF16),
            pltpu.SemaphoreType.DMA((6 + 2 * (f // 256),)),
        ],
        compiler_params=params(40),
        name="train",
    )(scal, blocks_a, blocks_b, x, gate_up, down)


def update_gate_kernel(eta, scal, x_a, x_b, bg_a, bg_b, gu_h, out, x, x_t, bg, w, stage, sem):
    slots = x.shape[1]
    wide = x.shape[2]
    groups, four, high, cols = stage.shape[1:]
    steps = stage.shape[0]
    mine = pl.ds(pl.multiple_of(scal[0] * wide, wide), wide)
    loads = [
        pltpu.make_async_copy(x_a.at[:, mine], x.at[0], sem.at[0]),
        pltpu.make_async_copy(x_b.at[:, mine], x.at[1], sem.at[1]),
        pltpu.make_async_copy(bg_a, bg.at[pl.ds(0, slots)], sem.at[2]),
        pltpu.make_async_copy(bg_b, bg.at[pl.ds(slots, slots)], sem.at[3]),
        pltpu.make_async_copy(gu_h.at[mine, :], w, sem.at[4]),
    ]
    for load in loads:
        load.start()
    for s in range(2):
        loads[s].wait()

        def turn(c, _):
            part = pl.ds(pl.multiple_of(c * 256, 256), 256)
            x_t[part, s * slots:(s + 1) * slots] = x[s, :, part].T
            return 0

        lax.fori_loop(0, wide // 256, turn, 0)
    for load in loads[2:]:
        load.wait()

    def save(n):
        return pltpu.make_async_copy(stage.at[n], out.at[:, :, pl.ds(pl.multiple_of(n * high, high), high), :], sem.at[5 + n])

    def one(n, _):
        part = pl.ds(pl.multiple_of(n * cols, cols), cols)
        grad = jnp.dot(x_t[...], bg[:, part], preferred_element_type=F32)
        new = (w[:, part].astype(F32) - eta * grad).astype(BF16)
        stage[n] = new.reshape(groups, four, high, cols)
        save(n).start()
        return 0

    lax.fori_loop(0, steps, one, 0)
    for n in range(steps):
        save(n).wait()


def update_gate(eta, scal, x_a, x_b, bg_a, bg_b, gate_up):
    slots, d = x_a.shape
    f2 = bg_a.shape[1]
    wide = d // 2
    high, cols = wide // 64, 256
    steps = f2 // cols
    tall = steps * high + (f2 // 2) // 16
    return pl.pallas_call(
        lambda *refs: update_gate_kernel(eta, *refs),
        out_shape=jax.ShapeDtypeStruct((16, 4, tall, cols), BF16),
        in_specs=[smem()] + [anywhere()] * 5,
        out_specs=anywhere(),
        scratch_shapes=[
            pltpu.VMEM((2, slots, wide), BF16), pltpu.VMEM((wide, 2 * slots), BF16),
            pltpu.VMEM((2 * slots, f2), BF16), pltpu.VMEM((wide, f2), BF16),
            pltpu.VMEM((steps, 16, 4, high, cols), BF16), pltpu.SemaphoreType.DMA((5 + steps,)),
        ],
        compiler_params=params(40),
        name="update_gate",
    )(scal, x_a, x_b, bg_a, bg_b, gate_up)


def update_down_kernel(eta, scal, hid_a, hid_b, og_a, og_b, dw_h, given, out, hid, hid_t, og, w, stage, sem):
    slots = hid.shape[1]
    wide = og.shape[1]
    steps, groups, high, cols = stage.shape
    base = out.shape[2] - high
    mine = pl.ds(pl.multiple_of(scal[0] * wide, wide), wide)
    loads = [
        pltpu.make_async_copy(hid_a, hid.at[0], sem.at[0]),
        pltpu.make_async_copy(hid_b, hid.at[1], sem.at[1]),
        pltpu.make_async_copy(og_a, og.at[pl.ds(0, slots)], sem.at[2]),
        pltpu.make_async_copy(og_b, og.at[pl.ds(slots, slots)], sem.at[3]),
        pltpu.make_async_copy(dw_h.at[:, mine], w, sem.at[4]),
    ]
    for load in loads:
        load.start()
    for s in range(2):
        loads[s].wait()

        def turn(c, _):
            part = pl.ds(pl.multiple_of(c * 256, 256), 256)
            hid_t[part, s * slots:(s + 1) * slots] = hid[s, :, part].T
            return 0

        lax.fori_loop(0, hid.shape[2] // 256, turn, 0)
    for load in loads[2:]:
        load.wait()

    def save(n):
        return pltpu.make_async_copy(stage.at[n], out.at[:, n, pl.ds(base, high), :], sem.at[5 + n])

    def one(n, _):
        part = pl.ds(pl.multiple_of(n * cols, cols), cols)
        grad = jnp.dot(hid_t[...], og[:, part], preferred_element_type=F32)
        new = (w[:, part].astype(F32) - eta * grad).astype(BF16)
        stage[n] = new.reshape(groups, high, cols)
        save(n).start()
        return 0

    lax.fori_loop(0, steps, one, 0)
    for n in range(steps):
        save(n).wait()


def update_down(eta, scal, hid_a, hid_b, og_a, og_b, down, given):
    slots, f = hid_a.shape
    wide = og_a.shape[1]
    cols = given.shape[3]
    steps = wide // cols
    high = f // 16
    return pl.pallas_call(
        lambda *refs: update_down_kernel(eta, *refs),
        out_shape=jax.ShapeDtypeStruct(given.shape, BF16),
        in_specs=[smem()] + [anywhere()] * 6,
        out_specs=anywhere(),
        scratch_shapes=[
            pltpu.VMEM((2, slots, f), BF16), pltpu.VMEM((f, 2 * slots), BF16),
            pltpu.VMEM((2 * slots, wide), BF16), pltpu.VMEM((f, wide), BF16),
            pltpu.VMEM((steps, 16, high, cols), BF16), pltpu.SemaphoreType.DMA((5 + steps,)),
        ],
        input_output_aliases={6: 0},
        compiler_params=params(40),
        name="update_down",
    )(scal, hid_a, hid_b, og_a, og_b, down, given)


def choose_kernel(slot_map, src, out, sem):
    count = out.shape[0]

    def copy(i):
        return pltpu.make_async_copy(src.at[slot_map[i]], out.at[i], sem.at[i])

    def start(i, _):
        copy(i).start()
        return 0

    def wait(i, _):
        copy(i).wait()
        return 0

    lax.fori_loop(0, count, start, 0)
    lax.fori_loop(0, count, wait, 0)


def choose(slot_map, pieces):
    return pl.pallas_call(
        choose_kernel,
        out_shape=jax.ShapeDtypeStruct(pieces.shape, BF16),
        in_specs=[smem(), anywhere()],
        out_specs=vmem(),
        scratch_shapes=[pltpu.SemaphoreType.DMA((pieces.shape[0],))],
        compiler_params=params(16),
        name="choose",
    )(slot_map, pieces)


def serve_kernel(scal, blocks_a, blocks_b, x_h, w_a, w_b, out, x, gu, dw, hid, sem):
    half = scal[0]
    d = x.shape[1]
    high, f2 = gu.shape[3:]
    f = f2 // 2
    fc, dc = 256, 512
    steps = f2 // fc
    deep = dw.shape[1]
    base = w_a.shape[2] - deep

    load_x = pltpu.make_async_copy(x_h, x, sem.at[0])

    def load_gu(s, n):
        src, place = ((w_a, half), (w_b, 1 - half))[s]
        return pltpu.make_async_copy(
            src.at[:, :, pl.ds(n * high, high), :], gu.at[place, :, :, :, pl.ds(n * fc, fc)], sem.at[1 + 2 * n + s]
        )

    def load_dw(s, n):
        src, place = ((w_a, half), (w_b, 1 - half))[s]
        cols = pl.ds(pl.multiple_of(place * (d // 2) + n * fc, fc), fc)
        return pltpu.make_async_copy(
            src.at[:, n, pl.ds(base, deep), :], dw.at[:, :, cols], sem.at[1 + 2 * steps + 2 * n + s]
        )

    load_x.start()
    for n in range(steps):
        for s in range(2):
            load_gu(s, n).start()
    for n in range(4):
        for s in range(2):
            load_dw(s, n).start()
    load_x.wait()
    kept, scale = kept_and_scale(x[:, :LANES], half, limit_of(1, scal, blocks_a, blocks_b))
    for n in range(steps):
        for s in range(2):
            load_gu(s, n).wait()

    def project(i, _):
        left = pl.ds(pl.multiple_of(i * fc, fc), fc)
        right = pl.ds(pl.multiple_of(f + i * fc, fc), fc)
        g = jnp.dot(x[...], gu[:, :, :, :, left].reshape(d, fc), preferred_element_type=F32)
        u = jnp.dot(x[...], gu[:, :, :, :, right].reshape(d, fc), preferred_element_type=F32)
        hid[:, left] = (g * jax.nn.sigmoid(g) * u).astype(BF16)
        return 0

    lax.fori_loop(0, f // fc, project, 0)
    for n in range(4):
        for s in range(2):
            load_dw(s, n).wait()

    def outputs(c, _):
        cols = pl.ds(pl.multiple_of(c * dc, dc), dc)
        o = jnp.dot(hid[...], dw[:, :, cols].reshape(f, dc), preferred_element_type=F32)
        out[:, cols] = jnp.where(kept, scale * o, 0.0).astype(BF16)
        return 0

    lax.fori_loop(0, d // dc, outputs, 0)


def serve(scal, blocks_a, blocks_b, x, w_a, w_b):
    slots, d = x.shape
    f = d * 3 // 8
    high = d // 2 // 64
    steps = 2 * f // 256
    return pl.pallas_call(
        serve_kernel,
        out_shape=jax.ShapeDtypeStruct((slots, d), BF16),
        in_specs=[smem(), smem(), smem()] + [anywhere()] * 3,
        out_specs=vmem(),
        scratch_shapes=[
            pltpu.VMEM((slots, d), BF16), pltpu.VMEM((2, 16, 4, high, 2 * f), BF16), pltpu.VMEM((16, f // 16, d), BF16),
            pltpu.VMEM((slots, f), BF16), pltpu.SemaphoreType.DMA((9 + 2 * steps,)),
        ],
        compiler_params=params(40),
        name="serve",
    )(scal, blocks_a, blocks_b, x, w_a, w_b)


def unpack_kernel(members, scal, route, t_own, t_recv, p_own, p_recv, out, low, high, sem):
    half = scal[0]

    @pl.when(half == 0)
    def _():
        pltpu.make_async_copy(t_own, low, sem.at[0]).start()
        pltpu.make_async_copy(t_recv, high, sem.at[1]).start()

    @pl.when(half == 1)
    def _():
        pltpu.make_async_copy(p_recv, low, sem.at[0]).start()
        pltpu.make_async_copy(p_own, high, sem.at[1]).start()

    target = route[...]
    rows = target.shape[1]
    order = order_of(target, members)
    eye = (iota((rows, rows), 0) == iota((rows, rows), 1)).astype(BF16)
    pair = jnp.where(iota((BOX, rows), 0) == 0, target, order).astype(F32).astype(BF16)
    column = lax.dot_general(eye, pair, NT, preferred_element_type=F32).astype(jnp.int32)
    goal, rank = column[:, 0:1], column[:, 1:2]
    slots = members * BOX
    at = iota((rows, slots), 1)
    pick_low = (at == jnp.where(rank < PART, goal * BOX + rank, -1)).astype(BF16)
    pick_high = (at == jnp.where(rank >= PART, goal * BOX + rank - PART, -1)).astype(BF16)
    pltpu.make_async_copy(t_own, low, sem.at[0]).wait()
    pltpu.make_async_copy(t_own, high, sem.at[1]).wait()
    total = jnp.dot(pick_low, low[...], preferred_element_type=F32)
    total = total + jnp.dot(pick_high, high[...], preferred_element_type=F32)
    out[...] = total.astype(BF16)


def unpack(members, scal, route, t_own, t_recv, p_own, p_recv):
    slots, d = t_own.shape
    rows = route.shape[1]
    return pl.pallas_call(
        lambda *refs: unpack_kernel(members, *refs),
        out_shape=jax.ShapeDtypeStruct((rows, d), BF16),
        in_specs=[smem(), vmem()] + [anywhere()] * 4,
        out_specs=vmem(),
        scratch_shapes=[pltpu.VMEM((slots, d), BF16), pltpu.VMEM((slots, d), BF16), pltpu.SemaphoreType.DMA((2,))],
        compiler_params=params(),
        name="unpack",
    )(scal, route, t_own, t_recv, p_own, p_recv)


def swap(value):
    return lax.ppermute(value, "half", SWAP)


def spread(value):
    return lax.all_to_all(value, "ep", split_axis=0, concat_axis=0, tiled=True)


def step(activations, routes, blocks, row_scale, gate_up, down_weight, slot_map):
    members = lax.axis_size("ep")
    tokens = activations[0]
    row_count, width = tokens.shape
    boxed = (members, BOX, width)
    flat = (members * BOX, width)
    route = routes.reshape(1, row_count)
    gate_up, down_weight = gate_up[0], down_weight[0]
    scal = jnp.stack([lax.axis_index("half"), lax.axis_index("ep")]).astype(jnp.int32)
    eta = 0.03 / math.sqrt(row_count)

    tokens_b, route_b, scale_b, blocks_b = swap(tokens), swap(route), swap(row_scale), swap(blocks)
    parts = (scal, tokens, tokens_b, route, route_b, row_scale, scale_b)
    train_rows = spread(pack(0, members, *parts).reshape(boxed)).reshape(flat)
    serve_rows = spread(pack(1, members, *parts).reshape(boxed)).reshape(flat)

    train_rows_b = swap(train_rows)
    hidden, grad_own, grad_send, both = train(scal, blocks, blocks_b, train_rows, gate_up, down_weight)
    both_b = swap(both)
    hidden_send, grad_send, _ = lax.optimization_barrier((hidden, grad_send, both_b))
    hidden_b, grad_b = swap(hidden_send), swap(grad_send)
    new = update_gate(eta, scal, train_rows, train_rows_b, both, both_b, gate_up)
    new = update_down(eta, scal, hidden, hidden_b, grad_own, grad_b, down_weight, new)
    laid = new.shape
    tiled = (members,) + laid[2:]
    pieces = spread(new.reshape(tiled))
    both, _ = lax.optimization_barrier((both, new))
    input_grad = lax.dot_general(both, gate_up, NT, preferred_element_type=F32).astype(BF16)
    chosen = choose(slot_map, pieces)
    slots = spread(chosen)
    input_grad, _ = lax.optimization_barrier((input_grad, slots))
    train_back = spread(input_grad.reshape(boxed)).reshape(flat)
    slots_b = swap(slots)
    served = serve(scal, blocks, blocks_b, serve_rows, slots.reshape(laid), slots_b.reshape(laid))
    serve_back = spread(served.reshape(boxed)).reshape(flat)
    train_other, serve_other = swap(train_back), swap(serve_back)
    return unpack(members, scal, route, train_back, train_other, serve_back, serve_other)[None]


def solution(mesh):
    placed = (
        P("half", "ep", None),
        P("half", "ep", None),
        P("half", None),
        P("half", "ep"),
        P("ep", None, None),
        P("ep", None, None),
        P(),
    )
    return jax.shard_map(step, mesh=mesh, in_specs=placed, out_specs=P("half", "ep", None), check_vma=False)
```

```python
import math

import jax
import jax.numpy as jnp
from jax import lax
from jax.experimental import pallas as pl
from jax.experimental.pallas import tpu as pltpu
from jax.sharding import PartitionSpec as P


BLK = 128
PART = 7
BOX = 8
COUNT = 8
LANES = 128
SWAP = [(0, 1), (1, 0)]
F32 = jnp.float32
BF16 = jnp.bfloat16
NT = (((1,), (1,)), ((), ()))


def params(mib=56):
    return pltpu.CompilerParams(vmem_limit_bytes=mib << 20)


def iota(shape, dim):
    return lax.broadcasted_iota(jnp.int32, shape, dim)


def anywhere():
    return pl.BlockSpec(memory_space=pl.ANY)


def in_hbm(*values):
    return [pltpu.with_memory_space_constraint(value, pltpu.HBM) for value in values]


def vmem():
    return pl.BlockSpec(memory_space=pltpu.VMEM)


def smem():
    return pl.BlockSpec(memory_space=pltpu.SMEM)


def order_of(target, members):
    rows = target.shape[1]
    named = iota((members, rows), 0) == target
    onehot = named.astype(BF16)
    upper = (iota((rows, rows), 0) < iota((rows, rows), 1)).astype(BF16)
    before = jnp.dot(onehot, upper, preferred_element_type=F32)
    return jnp.sum(jnp.where(named, before, 0.0), axis=0, keepdims=True).astype(jnp.int32)


def pack_kernel(group, members, scal, tok_a, tok_b, route_a, route_b, scale_a, scale_b, out, tok, sem):
    half = scal[0]
    own = half == group

    @pl.when(own)
    def _():
        pltpu.make_async_copy(tok_a, tok, sem).start()

    @pl.when(jnp.logical_not(own))
    def _():
        pltpu.make_async_copy(tok_b, tok, sem).start()

    target = jnp.where(own, route_a[...], route_b[...])
    scale = jnp.where(own, scale_a[...].astype(F32), scale_b[...].astype(F32))
    rows = target.shape[1]
    slots = members * BOX
    order = order_of(target, members) - PART * half
    inside = (order >= 0) & (order < PART)
    place = jnp.where(inside, target * BOX + order, -1)
    placer = (iota((slots, rows), 0) == place).astype(BF16)
    tags = (iota((slots, rows), 0) == target * BOX + PART).astype(BF16)
    lane = iota((LANES, rows), 0)
    told = jnp.where((lane == order) & inside, scale, jnp.where(lane == COUNT, 1.0, 0.0)).astype(BF16)
    info = lax.dot_general(tags, told, NT, preferred_element_type=F32)
    pltpu.make_async_copy(tok_a, tok, sem).wait()
    first = jnp.dot(placer, tok[:, :LANES], preferred_element_type=F32) + info
    out[:, :LANES] = first.astype(BF16)
    out[:, LANES:] = jnp.dot(placer, tok[:, LANES:], preferred_element_type=F32).astype(BF16)


def pack(group, members, scal, tok_a, tok_b, route_a, route_b, scale_a, scale_b):
    slots = members * BOX
    width = tok_a.shape[1]
    return pl.pallas_call(
        lambda *refs: pack_kernel(group, members, *refs),
        out_shape=pltpu.HBM((slots, width), BF16),
        in_specs=[smem(), anywhere(), anywhere(), vmem(), vmem(), vmem(), vmem()],
        out_specs=vmem(),
        scratch_shapes=[pltpu.VMEM(tok_a.shape, BF16), pltpu.SemaphoreType.DMA],
        compiler_params=params(24),
    )(scal, tok_a, tok_b, route_a, route_b, scale_a, scale_b)


def kept_and_scale(head, half, limit):
    slots = head.shape[0]
    row = iota((slots, slots), 0) // BOX
    col = iota((slots, slots), 1)
    tag = (col % BOX) == PART
    mine = (tag & (col // BOX == row)).astype(BF16)
    lower = (tag & (col // BOX < row)).astype(BF16)
    here = jnp.dot(mine, head, preferred_element_type=F32)
    below = jnp.dot(lower, head, preferred_element_type=F32)
    lane = iota((slots, LANES), 1)
    place = iota((slots, LANES), 0) % BOX
    scale = jnp.sum(jnp.where(lane == place, here, 0.0), axis=1, keepdims=True)
    total = jnp.sum(jnp.where(lane == COUNT, here, 0.0), axis=1, keepdims=True)
    ahead = jnp.sum(jnp.where(lane == COUNT, below, 0.0), axis=1, keepdims=True)
    k = iota((slots, 1), 0) % BOX
    index = (k + PART * half).astype(F32)
    kept = (k < PART) & (index < total) & (ahead + index < limit.astype(F32))
    return kept, scale


def limit_of(group, scal, blocks_a, blocks_b):
    own = scal[0] == group
    at = scal[1]
    return jnp.where(own, blocks_a[0, at], blocks_b[0, at]) * BLK


def train_kernel(scal, blocks_a, blocks_b, x_h, gu_h, dw_h, hid_h, og_own, og_send, bg_h,
                 x, gu, dw, gate, up, hid, hid_t, og, bg, sem):
    half = scal[0]
    d, f2 = gu.shape
    f = f2 // 2
    fc, dc = 256, 512
    nf, nd = f // fc, d // dc

    def load_gu(i, which):
        cols = pl.ds(pl.multiple_of(which * f + i * fc, fc), fc)
        return pltpu.make_async_copy(gu_h.at[:, cols], gu.at[:, cols], sem.at[2 + 2 * i + which])

    load_x = pltpu.make_async_copy(x_h, x, sem.at[0])
    load_dw = pltpu.make_async_copy(dw_h, dw, sem.at[1])
    load_x.start()
    for i in range(nf):
        load_gu(i, 0).start()
        load_gu(i, 1).start()
    load_dw.start()
    load_x.wait()
    kept, scale = kept_and_scale(x[:, :LANES], half, limit_of(0, scal, blocks_a, blocks_b))
    keep = jnp.where(kept, 1.0, 0.0)

    def project(i, _):
        load_gu(i, 0).wait()
        load_gu(i, 1).wait()
        left = pl.ds(pl.multiple_of(i * fc, fc), fc)
        right = pl.ds(pl.multiple_of(f + i * fc, fc), fc)
        g = jnp.dot(x[...], gu[:, left], preferred_element_type=F32)
        u = jnp.dot(x[...], gu[:, right], preferred_element_type=F32)
        gate[:, left] = g
        up[:, left] = u
        h = (keep * (g * jax.nn.sigmoid(g) * u)).astype(BF16)
        hid[:, left] = h
        hid_t[left, :] = h.T
        return 0

    lax.fori_loop(0, nf, project, 0)
    out_hid = pltpu.make_async_copy(hid_t, hid_h, sem.at[2 + 2 * nf])
    out_hid.start()
    load_dw.wait()

    def outputs(c, _):
        cols = pl.ds(pl.multiple_of(c * dc, dc), dc)
        o = jnp.dot(hid[...], dw[:, cols], preferred_element_type=F32)
        og[:, cols] = (scale * o).astype(BF16)
        return 0

    lax.fori_loop(0, nd, outputs, 0)

    def out_og(which, place):
        cols = pl.ds(pl.multiple_of(place * (d // 2), d // 2), d // 2)
        return pltpu.make_async_copy(og.at[:, cols], (og_own, og_send)[which], sem.at[3 + 2 * nf + which])

    out_og(0, half).start()
    out_og(1, 1 - half).start()

    def hidden_back(i, _):
        left = pl.ds(pl.multiple_of(i * fc, fc), fc)
        right = pl.ds(pl.multiple_of(f + i * fc, fc), fc)
        hg = lax.dot_general(og[...], dw[left, :], NT, preferred_element_type=F32)
        g = gate[:, left]
        s = jax.nn.sigmoid(g)
        bg[:, left] = (hg * up[:, left] * (s * (1.0 + g * (1.0 - s)))).astype(BF16)
        bg[:, right] = (hg * (g * s)).astype(BF16)
        return 0

    lax.fori_loop(0, nf, hidden_back, 0)
    out_bg = pltpu.make_async_copy(bg, bg_h, sem.at[5 + 2 * nf])
    out_bg.start()
    out_hid.wait()
    out_og(0, half).wait()
    out_og(1, 1 - half).wait()
    out_bg.wait()


def train(scal, blocks_a, blocks_b, x, gate_up, down):
    slots, d = x.shape
    f2 = gate_up.shape[1]
    f = f2 // 2
    half_rows = jax.ShapeDtypeStruct((slots, d // 2), BF16)
    return pl.pallas_call(
        train_kernel,
        out_shape=(
            jax.ShapeDtypeStruct((f, slots), BF16), half_rows, half_rows, pltpu.HBM((slots, f2), BF16)
        ),
        in_specs=[smem(), smem(), smem(), anywhere(), anywhere(), anywhere()],
        out_specs=(anywhere(),) * 4,
        scratch_shapes=[
            pltpu.VMEM((slots, d), BF16), pltpu.VMEM((d, f2), BF16), pltpu.VMEM((f, d), BF16),
            pltpu.VMEM((slots, f), F32), pltpu.VMEM((slots, f), F32), pltpu.VMEM((slots, f), BF16),
            pltpu.VMEM((f, slots), BF16), pltpu.VMEM((slots, d), BF16), pltpu.VMEM((slots, f2), BF16),
            pltpu.SemaphoreType.DMA((6 + 2 * (f // 256),)),
        ],
        compiler_params=params(40),
        name="train",
    )(scal, blocks_a, blocks_b, x, gate_up, down)


def turn_kernel(scal, x_a, x_b, out, x, sem):
    slots, wide = x.shape[1:]
    mine = pl.ds(pl.multiple_of(scal[0] * wide, wide), wide)
    loads = [pltpu.make_async_copy(src.at[:, mine], x.at[s], sem.at[s]) for s, src in enumerate((x_a, x_b))]
    for load in loads:
        load.start()
    for s in range(2):
        loads[s].wait()

        def turn(c, _):
            part = pl.ds(pl.multiple_of(c * 256, 256), 256)
            out[part, s * slots:(s + 1) * slots] = x[s, :, part].T
            return 0

        lax.fori_loop(0, wide // 256, turn, 0)


def turned(scal, x_a, x_b):
    slots, d = x_a.shape
    wide = d // 2
    return pl.pallas_call(
        turn_kernel,
        out_shape=jax.ShapeDtypeStruct((wide, 2 * slots), BF16),
        in_specs=[smem(), anywhere(), anywhere()],
        out_specs=vmem(),
        scratch_shapes=[pltpu.VMEM((2, slots, wide), BF16), pltpu.SemaphoreType.DMA((2,))],
        compiler_params=params(12),
        name="turn",
    )(scal, x_a, x_b)


def update_gate_kernel(eta, scal, xt_h, bg_a, bg_b, gu_h, out, x_t, bg, w, stage, sem):
    wide = x_t.shape[0]
    slots = x_t.shape[1] // 2
    groups, four, high, cols = stage.shape[1:]
    steps = stage.shape[0]
    mine = pl.ds(pl.multiple_of(scal[0] * wide, wide), wide)
    load_x = pltpu.make_async_copy(xt_h, x_t, sem.at[0])

    def part(n):
        return pl.ds(pl.multiple_of(n * cols, cols), cols)

    def loads(n):
        return (
            pltpu.make_async_copy(bg_a.at[:, part(n)], bg.at[pl.ds(0, slots), part(n)], sem.at[1 + 3 * n]),
            pltpu.make_async_copy(bg_b.at[:, part(n)], bg.at[pl.ds(slots, slots), part(n)], sem.at[2 + 3 * n]),
            pltpu.make_async_copy(gu_h.at[mine, part(n)], w.at[:, part(n)], sem.at[3 + 3 * n]),
        )

    def save(n):
        rows = pl.ds(pl.multiple_of(n * high, high), high)
        return pltpu.make_async_copy(stage.at[n], out.at[:, :, rows, :], sem.at[1 + 3 * steps + n])

    load_x.start()
    for n in range(steps):
        for load in loads(n):
            load.start()
    load_x.wait()

    def one(n, _):
        for load in loads(n):
            load.wait()
        grad = jnp.dot(x_t[...], bg[:, part(n)], preferred_element_type=F32)
        new = (w[:, part(n)].astype(F32) - eta * grad).astype(BF16)
        stage[n] = new.reshape(groups, four, high, cols)
        save(n).start()
        return 0

    lax.fori_loop(0, steps, one, 0)
    for n in range(steps):
        save(n).wait()


def update_gate(eta, scal, x_t, bg_a, bg_b, gate_up):
    wide, both = x_t.shape
    f2 = bg_a.shape[1]
    high, cols = wide // 64, 256
    steps = f2 // cols
    tall = steps * high + (f2 // 2) // 16
    return pl.pallas_call(
        lambda *refs: update_gate_kernel(eta, *refs),
        out_shape=pltpu.HBM((16, 4, tall, cols), BF16),
        in_specs=[smem()] + [anywhere()] * 4,
        out_specs=anywhere(),
        scratch_shapes=[
            pltpu.VMEM((wide, both), BF16), pltpu.VMEM((both, f2), BF16), pltpu.VMEM((wide, f2), BF16),
            pltpu.VMEM((steps, 16, 4, high, cols), BF16), pltpu.SemaphoreType.DMA((1 + 4 * steps,)),
        ],
        compiler_params=params(32),
        name="update_gate",
    )(scal, x_t, bg_a, bg_b, gate_up)


def update_down_kernel(eta, scal, hid_a, hid_b, og_a, og_b, dw_h, given, out, hid_t, og, w, stage, sem):
    slots = hid_t.shape[1] // 2
    wide = og.shape[1]
    steps, groups, high, cols = stage.shape
    base = out.shape[2] - high
    mine = pl.ds(pl.multiple_of(scal[0] * wide, wide), wide)
    loads = [
        pltpu.make_async_copy(hid_a, hid_t.at[:, pl.ds(0, slots)], sem.at[0]),
        pltpu.make_async_copy(hid_b, hid_t.at[:, pl.ds(slots, slots)], sem.at[1]),
        pltpu.make_async_copy(og_a, og.at[pl.ds(0, slots)], sem.at[2]),
        pltpu.make_async_copy(og_b, og.at[pl.ds(slots, slots)], sem.at[3]),
        pltpu.make_async_copy(dw_h.at[:, mine], w, sem.at[4]),
    ]
    for load in loads:
        load.start()
    for load in loads:
        load.wait()

    def save(n):
        return pltpu.make_async_copy(stage.at[n], out.at[:, n, pl.ds(base, high), :], sem.at[5 + n])

    def one(n, _):
        part = pl.ds(pl.multiple_of(n * cols, cols), cols)
        grad = jnp.dot(hid_t[...], og[:, part], preferred_element_type=F32)
        new = (w[:, part].astype(F32) - eta * grad).astype(BF16)
        stage[n] = new.reshape(groups, high, cols)
        save(n).start()
        return 0

    lax.fori_loop(0, steps, one, 0)
    for n in range(steps):
        save(n).wait()


def update_down(eta, scal, hid_a, hid_b, og_a, og_b, down, given):
    f, slots = hid_a.shape
    wide = og_a.shape[1]
    cols = given.shape[3]
    steps = wide // cols
    high = f // 16
    return pl.pallas_call(
        lambda *refs: update_down_kernel(eta, *refs),
        out_shape=pltpu.HBM(given.shape, BF16),
        in_specs=[smem()] + [anywhere()] * 6,
        out_specs=anywhere(),
        scratch_shapes=[
            pltpu.VMEM((f, 2 * slots), BF16), pltpu.VMEM((2 * slots, wide), BF16), pltpu.VMEM((f, wide), BF16),
            pltpu.VMEM((steps, 16, high, cols), BF16), pltpu.SemaphoreType.DMA((5 + steps,)),
        ],
        input_output_aliases={6: 0},
        compiler_params=params(24),
        name="update_down",
    )(scal, hid_a, hid_b, og_a, og_b, down, given)


def choose_kernel(slot_map, src, out, sem):
    count = out.shape[0]

    def copy(i):
        return pltpu.make_async_copy(src.at[slot_map[i]], out.at[i], sem.at[i])

    def start(i, _):
        copy(i).start()
        return 0

    def wait(i, _):
        copy(i).wait()
        return 0

    lax.fori_loop(0, count, start, 0)
    lax.fori_loop(0, count, wait, 0)


def choose(slot_map, pieces):
    return pl.pallas_call(
        choose_kernel,
        out_shape=jax.ShapeDtypeStruct(pieces.shape, BF16),
        in_specs=[smem(), anywhere()],
        out_specs=vmem(),
        scratch_shapes=[pltpu.SemaphoreType.DMA((pieces.shape[0],))],
        compiler_params=params(16),
        name="choose",
    )(slot_map, pieces)


def serve_kernel(scal, blocks_a, blocks_b, x_h, w_a, w_b, out, x, gu, dw, hid, sem):
    half = scal[0]
    d = x.shape[1]
    high, f2 = gu.shape[3:]
    f = f2 // 2
    fc, dc = 256, 512
    steps = f2 // fc
    deep = dw.shape[1]
    base = w_a.shape[2] - deep

    load_x = pltpu.make_async_copy(x_h, x, sem.at[0])

    def load_gu(s, n):
        src, place = ((w_a, half), (w_b, 1 - half))[s]
        return pltpu.make_async_copy(
            src.at[:, :, pl.ds(n * high, high), :], gu.at[place, :, :, :, pl.ds(n * fc, fc)], sem.at[1 + 2 * n + s]
        )

    def load_dw(s, n):
        src, place = ((w_a, half), (w_b, 1 - half))[s]
        cols = pl.ds(pl.multiple_of(place * (d // 2) + n * fc, fc), fc)
        return pltpu.make_async_copy(
            src.at[:, n, pl.ds(base, deep), :], dw.at[:, :, cols], sem.at[1 + 2 * steps + 2 * n + s]
        )

    load_x.start()
    for n in range(steps):
        for s in range(2):
            load_gu(s, n).start()
    for n in range(4):
        for s in range(2):
            load_dw(s, n).start()
    load_x.wait()
    kept, scale = kept_and_scale(x[:, :LANES], half, limit_of(1, scal, blocks_a, blocks_b))
    for n in range(steps):
        for s in range(2):
            load_gu(s, n).wait()

    def project(i, _):
        left = pl.ds(pl.multiple_of(i * fc, fc), fc)
        right = pl.ds(pl.multiple_of(f + i * fc, fc), fc)
        g = jnp.dot(x[...], gu[:, :, :, :, left].reshape(d, fc), preferred_element_type=F32)
        u = jnp.dot(x[...], gu[:, :, :, :, right].reshape(d, fc), preferred_element_type=F32)
        hid[:, left] = (g * jax.nn.sigmoid(g) * u).astype(BF16)
        return 0

    lax.fori_loop(0, f // fc, project, 0)
    for n in range(4):
        for s in range(2):
            load_dw(s, n).wait()

    def outputs(c, _):
        cols = pl.ds(pl.multiple_of(c * dc, dc), dc)
        o = jnp.dot(hid[...], dw[:, :, cols].reshape(f, dc), preferred_element_type=F32)
        out[:, cols] = jnp.where(kept, scale * o, 0.0).astype(BF16)
        return 0

    lax.fori_loop(0, d // dc, outputs, 0)


def serve(scal, blocks_a, blocks_b, x, w_a, w_b):
    slots, d = x.shape
    f = d * 3 // 8
    high = d // 2 // 64
    steps = 2 * f // 256
    return pl.pallas_call(
        serve_kernel,
        out_shape=pltpu.HBM((slots, d), BF16),
        in_specs=[smem(), smem(), smem()] + [anywhere()] * 3,
        out_specs=vmem(),
        scratch_shapes=[
            pltpu.VMEM((slots, d), BF16), pltpu.VMEM((2, 16, 4, high, 2 * f), BF16), pltpu.VMEM((16, f // 16, d), BF16),
            pltpu.VMEM((slots, f), BF16), pltpu.SemaphoreType.DMA((9 + 2 * steps,)),
        ],
        compiler_params=params(40),
        name="serve",
    )(scal, blocks_a, blocks_b, x, w_a, w_b)


def unpack_kernel(members, scal, route, t_own, t_recv, p_own, p_recv, out, low, high, sem):
    half = scal[0]

    @pl.when(half == 0)
    def _():
        pltpu.make_async_copy(t_own, low, sem.at[0]).start()
        pltpu.make_async_copy(t_recv, high, sem.at[1]).start()

    @pl.when(half == 1)
    def _():
        pltpu.make_async_copy(p_recv, low, sem.at[0]).start()
        pltpu.make_async_copy(p_own, high, sem.at[1]).start()

    target = route[...]
    rows = target.shape[1]
    order = order_of(target, members)
    eye = (iota((rows, rows), 0) == iota((rows, rows), 1)).astype(BF16)
    pair = jnp.where(iota((BOX, rows), 0) == 0, target, order).astype(F32).astype(BF16)
    column = lax.dot_general(eye, pair, NT, preferred_element_type=F32).astype(jnp.int32)
    goal, rank = column[:, 0:1], column[:, 1:2]
    slots = members * BOX
    at = iota((rows, slots), 1)
    pick_low = (at == jnp.where(rank < PART, goal * BOX + rank, -1)).astype(BF16)
    pick_high = (at == jnp.where(rank >= PART, goal * BOX + rank - PART, -1)).astype(BF16)
    pltpu.make_async_copy(t_own, low, sem.at[0]).wait()
    pltpu.make_async_copy(t_own, high, sem.at[1]).wait()
    total = jnp.dot(pick_low, low[...], preferred_element_type=F32)
    total = total + jnp.dot(pick_high, high[...], preferred_element_type=F32)
    out[...] = total.astype(BF16)


def unpack(members, scal, route, t_own, t_recv, p_own, p_recv):
    slots, d = t_own.shape
    rows = route.shape[1]
    return pl.pallas_call(
        lambda *refs: unpack_kernel(members, *refs),
        out_shape=jax.ShapeDtypeStruct((rows, d), BF16),
        in_specs=[smem(), vmem()] + [anywhere()] * 4,
        out_specs=vmem(),
        scratch_shapes=[pltpu.VMEM((slots, d), BF16), pltpu.VMEM((slots, d), BF16), pltpu.SemaphoreType.DMA((2,))],
        compiler_params=params(24),
        name="unpack",
    )(scal, route, t_own, t_recv, p_own, p_recv)


def swap(value):
    return lax.ppermute(value, "half", SWAP)


def spread(value):
    return lax.all_to_all(value, "ep", split_axis=0, concat_axis=0, tiled=True)


def step(activations, routes, blocks, row_scale, gate_up, down_weight, slot_map):
    members = lax.axis_size("ep")
    tokens = activations[0]
    row_count, width = tokens.shape
    boxed = (members, BOX, width)
    flat = (members * BOX, width)
    route = routes.reshape(1, row_count)
    gate_up, down_weight = gate_up[0], down_weight[0]
    scal = jnp.stack([lax.axis_index("half"), lax.axis_index("ep")]).astype(jnp.int32)
    eta = 0.03 / math.sqrt(row_count)

    gate_h, down_h = in_hbm(gate_up, down_weight)
    tokens_b, route_b, scale_b, blocks_b = swap(tokens), swap(route), swap(row_scale), swap(blocks)
    parts = (scal, *in_hbm(tokens), tokens_b, *in_hbm(route), route_b, *in_hbm(row_scale), scale_b)
    train_rows = spread(pack(0, members, *parts).reshape(boxed)).reshape(flat)
    packed = pack(1, members, *parts)
    serve_rows = spread(packed.reshape(boxed)).reshape(flat)

    train_rows_b = swap(train_rows)
    hidden, grad_own, grad_send, both = train(scal, blocks, blocks_b, train_rows, gate_h, down_h)
    both_b = swap(both)
    rows_t = turned(scal, train_rows, train_rows_b)
    hidden_send, grad_send, _ = lax.optimization_barrier((hidden, grad_send, both_b))
    hidden_b = swap(hidden_send)
    grad_b = swap(grad_send)
    new = update_gate(eta, scal, rows_t, both, both_b, gate_h)
    new = update_down(eta, scal, hidden, hidden_b, grad_own, grad_b, down_h, new)
    laid = new.shape
    tiled = (members,) + laid[2:]
    pieces = spread(new.reshape(tiled))
    both, _ = lax.optimization_barrier((both, new))
    input_grad = lax.dot_general(both, gate_up, NT, preferred_element_type=F32).astype(BF16)
    chosen = choose(slot_map, pieces)
    slots = spread(chosen)
    input_grad, _ = lax.optimization_barrier((input_grad, slots))
    train_back = spread(input_grad.reshape(boxed)).reshape(flat)
    slots_b = swap(slots)
    served = serve(scal, blocks, blocks_b, serve_rows, slots.reshape(laid), slots_b.reshape(laid))
    serve_back = spread(served.reshape(boxed)).reshape(flat)
    train_other, serve_other = swap(train_back), swap(serve_back)
    return unpack(members, scal, route, train_back, train_other, serve_back, serve_other)[None]


def solution(mesh):
    placed = (
        P("half", "ep", None),
        P("half", "ep", None),
        P("half", None),
        P("half", "ep"),
        P("ep", None, None),
        P("ep", None, None),
        P(),
    )
    return jax.shard_map(step, mesh=mesh, in_specs=placed, out_specs=P("half", "ep", None), check_vma=False)
```

```python
import math

import jax
import jax.numpy as jnp
from jax import lax
from jax.experimental import pallas as pl
from jax.experimental.pallas import tpu as pltpu
from jax.sharding import PartitionSpec as P


BLK = 128
PART = 7
BOX = 8
COUNT = 8
LANES = 128
SWAP = [(0, 1), (1, 0)]
F32 = jnp.float32
BF16 = jnp.bfloat16
NT = (((1,), (1,)), ((), ()))


def params(mib=56):
    return pltpu.CompilerParams(vmem_limit_bytes=mib << 20)


def iota(shape, dim):
    return lax.broadcasted_iota(jnp.int32, shape, dim)


def anywhere():
    return pl.BlockSpec(memory_space=pl.ANY)


def in_hbm(*values):
    return [pltpu.with_memory_space_constraint(value, pltpu.HBM) for value in values]


def vmem():
    return pl.BlockSpec(memory_space=pltpu.VMEM)


def smem():
    return pl.BlockSpec(memory_space=pltpu.SMEM)


def order_of(target, members):
    rows = target.shape[1]
    named = iota((members, rows), 0) == target
    onehot = named.astype(BF16)
    upper = (iota((rows, rows), 0) < iota((rows, rows), 1)).astype(BF16)
    before = jnp.dot(onehot, upper, preferred_element_type=F32)
    return jnp.sum(jnp.where(named, before, 0.0), axis=0, keepdims=True).astype(jnp.int32)


def prepare_kernel(members, scal, route_a, route_b, scale_a, scale_b, train_p, train_i, serve_p, serve_i, own_p, recv_p):
    half = scal[0]
    slots = members * BOX
    rows = route_a.shape[1]
    order_a, order_b = order_of(route_a[...], members), order_of(route_b[...], members)
    for group, placer, info in ((0, train_p, train_i), (1, serve_p, serve_i)):
        own = half == group
        target = jnp.where(own, route_a[...], route_b[...])
        scale = jnp.where(own, scale_a[...].astype(F32), scale_b[...].astype(F32))
        order = jnp.where(own, order_a, order_b) - PART * half
        inside = (order >= 0) & (order < PART)
        place = jnp.where(inside, target * BOX + order, -1)
        placer[...] = (iota((slots, rows), 0) == place).astype(BF16)
        tags = (iota((slots, rows), 0) == target * BOX + PART).astype(BF16)
        lane = iota((LANES, rows), 0)
        told = jnp.where((lane == order) & inside, scale, jnp.where(lane == COUNT, 1.0, 0.0)).astype(BF16)
        info[...] = lax.dot_general(tags, told, NT, preferred_element_type=F32).astype(BF16)
    eye = (iota((rows, rows), 0) == iota((rows, rows), 1)).astype(BF16)
    pair = jnp.where(iota((BOX, rows), 0) == 0, route_a[...], order_a).astype(F32).astype(BF16)
    column = lax.dot_general(eye, pair, NT, preferred_element_type=F32).astype(jnp.int32)
    goal, rank = column[:, 0:1], column[:, 1:2]
    for first, pick in ((PART * half, own_p), (PART * (1 - half), recv_p)):
        k = rank - first
        at = jnp.where((k >= 0) & (k < PART), goal * BOX + k, -1)
        pick[...] = (iota((rows, slots), 1) == at).astype(BF16)


def prepare(members, scal, route_a, route_b, scale_a, scale_b):
    rows = route_a.shape[1]
    slots = members * BOX
    placer = jax.ShapeDtypeStruct((slots, rows), BF16)
    info = jax.ShapeDtypeStruct((slots, LANES), BF16)
    pick = jax.ShapeDtypeStruct((rows, slots), BF16)
    return pl.pallas_call(
        lambda *refs: prepare_kernel(members, *refs),
        out_shape=(placer, info, placer, info, pick, pick),
        in_specs=[smem()] + [vmem()] * 4,
        out_specs=(vmem(),) * 6,
        compiler_params=params(16),
        name="prepare",
    )(scal, route_a, route_b, scale_a, scale_b)


def pack_kernel(group, scal, tok_a, tok_b, placer, info, out, tok, packed, sem):
    own = scal[0] == group
    wide = tok.shape[2]
    steps = tok.shape[0]

    def load(src, c):
        return pltpu.make_async_copy(src.at[:, pl.ds(c * wide, wide)], tok.at[c], sem.at[c])

    def save(c):
        return pltpu.make_async_copy(packed.at[c], out.at[:, pl.ds(c * wide, wide)], sem.at[steps + c])

    @pl.when(own)
    def _():
        for c in range(steps):
            load(tok_a, c).start()

    @pl.when(jnp.logical_not(own))
    def _():
        for c in range(steps):
            load(tok_b, c).start()

    for c in range(steps):
        load(tok_a, c).wait()
        box = jnp.dot(placer[...], tok[c], preferred_element_type=F32)
        if c == 0:
            packed[c, :, :LANES] = (box[:, :LANES] + info[...].astype(F32)).astype(BF16)
            packed[c, :, LANES:] = box[:, LANES:].astype(BF16)
        else:
            packed[c] = box.astype(BF16)
        save(c).start()
    for c in range(steps):
        save(c).wait()


def pack(group, scal, tok_a, tok_b, placer, info):
    slots, rows = placer.shape
    width = tok_a.shape[1]
    steps = 4
    return pl.pallas_call(
        lambda *refs: pack_kernel(group, *refs),
        out_shape=pltpu.HBM((slots, width), BF16),
        in_specs=[smem(), anywhere(), anywhere(), vmem(), vmem()],
        out_specs=anywhere(),
        scratch_shapes=[
            pltpu.VMEM((steps, rows, width // steps), BF16), pltpu.VMEM((steps, slots, width // steps), BF16),
            pltpu.SemaphoreType.DMA((2 * steps,)),
        ],
        compiler_params=params(16),
    )(scal, tok_a, tok_b, placer, info)


def kept_and_scale(head, half, limit):
    slots = head.shape[0]
    row = iota((slots, slots), 0) // BOX
    col = iota((slots, slots), 1)
    tag = (col % BOX) == PART
    mine = (tag & (col // BOX == row)).astype(BF16)
    lower = (tag & (col // BOX < row)).astype(BF16)
    here = jnp.dot(mine, head, preferred_element_type=F32)
    below = jnp.dot(lower, head, preferred_element_type=F32)
    lane = iota((slots, LANES), 1)
    place = iota((slots, LANES), 0) % BOX
    scale = jnp.sum(jnp.where(lane == place, here, 0.0), axis=1, keepdims=True)
    total = jnp.sum(jnp.where(lane == COUNT, here, 0.0), axis=1, keepdims=True)
    ahead = jnp.sum(jnp.where(lane == COUNT, below, 0.0), axis=1, keepdims=True)
    k = iota((slots, 1), 0) % BOX
    index = (k + PART * half).astype(F32)
    kept = (k < PART) & (index < total) & (ahead + index < limit.astype(F32))
    return kept, scale


def limit_of(group, scal, blocks_a, blocks_b):
    own = scal[0] == group
    at = scal[1]
    return jnp.where(own, blocks_a[0, at], blocks_b[0, at]) * BLK


def train_kernel(scal, blocks_a, blocks_b, x_h, gu_h, dw_h, hid_h, og_own, og_send, bg_h,
                 x, gu, dw, gate, up, hid, hid_t, og, bg, sem):
    half = scal[0]
    d, f2 = gu.shape
    f = f2 // 2
    fc, dc = 256, 512
    nf, nd = f // fc, d // dc

    def load_gu(i, which):
        cols = pl.ds(pl.multiple_of(which * f + i * fc, fc), fc)
        return pltpu.make_async_copy(gu_h.at[:, cols], gu.at[:, cols], sem.at[2 + 2 * i + which])

    load_x = pltpu.make_async_copy(x_h, x, sem.at[0])
    load_dw = pltpu.make_async_copy(dw_h, dw, sem.at[1])
    load_x.start()
    for i in range(nf):
        load_gu(i, 0).start()
        load_gu(i, 1).start()
    load_dw.start()
    load_x.wait()
    kept, scale = kept_and_scale(x[:, :LANES], half, limit_of(0, scal, blocks_a, blocks_b))
    keep = jnp.where(kept, 1.0, 0.0)

    def project(i, _):
        load_gu(i, 0).wait()
        load_gu(i, 1).wait()
        left = pl.ds(pl.multiple_of(i * fc, fc), fc)
        right = pl.ds(pl.multiple_of(f + i * fc, fc), fc)
        g = jnp.dot(x[...], gu[:, left], preferred_element_type=F32)
        u = jnp.dot(x[...], gu[:, right], preferred_element_type=F32)
        gate[:, left] = g
        up[:, left] = u
        h = (keep * (g * jax.nn.sigmoid(g) * u)).astype(BF16)
        hid[:, left] = h
        hid_t[left, :] = h.T
        return 0

    lax.fori_loop(0, nf, project, 0)
    out_hid = pltpu.make_async_copy(hid_t, hid_h, sem.at[2 + 2 * nf])
    out_hid.start()
    load_dw.wait()

    def outputs(c, _):
        cols = pl.ds(pl.multiple_of(c * dc, dc), dc)
        o = jnp.dot(hid[...], dw[:, cols], preferred_element_type=F32)
        og[:, cols] = (scale * o).astype(BF16)
        return 0

    lax.fori_loop(0, nd, outputs, 0)

    def out_og(which, place):
        cols = pl.ds(pl.multiple_of(place * (d // 2), d // 2), d // 2)
        return pltpu.make_async_copy(og.at[:, cols], (og_own, og_send)[which], sem.at[3 + 2 * nf + which])

    out_og(0, half).start()
    out_og(1, 1 - half).start()

    def hidden_back(i, _):
        left = pl.ds(pl.multiple_of(i * fc, fc), fc)
        right = pl.ds(pl.multiple_of(f + i * fc, fc), fc)
        hg = lax.dot_general(og[...], dw[left, :], NT, preferred_element_type=F32)
        g = gate[:, left]
        s = jax.nn.sigmoid(g)
        bg[:, left] = (hg * up[:, left] * (s * (1.0 + g * (1.0 - s)))).astype(BF16)
        bg[:, right] = (hg * (g * s)).astype(BF16)
        return 0

    lax.fori_loop(0, nf, hidden_back, 0)
    out_bg = pltpu.make_async_copy(bg, bg_h, sem.at[5 + 2 * nf])
    out_bg.start()
    out_hid.wait()
    out_og(0, half).wait()
    out_og(1, 1 - half).wait()
    out_bg.wait()


def train(scal, blocks_a, blocks_b, x, gate_up, down):
    slots, d = x.shape
    f2 = gate_up.shape[1]
    f = f2 // 2
    half_rows = jax.ShapeDtypeStruct((slots, d // 2), BF16)
    return pl.pallas_call(
        train_kernel,
        out_shape=(
            jax.ShapeDtypeStruct((f, slots), BF16), half_rows, half_rows, pltpu.HBM((slots, f2), BF16)
        ),
        in_specs=[smem(), smem(), smem(), anywhere(), anywhere(), anywhere()],
        out_specs=(anywhere(),) * 4,
        scratch_shapes=[
            pltpu.VMEM((slots, d), BF16), pltpu.VMEM((d, f2), BF16), pltpu.VMEM((f, d), BF16),
            pltpu.VMEM((slots, f), F32), pltpu.VMEM((slots, f), F32), pltpu.VMEM((slots, f), BF16),
            pltpu.VMEM((f, slots), BF16), pltpu.VMEM((slots, d), BF16), pltpu.VMEM((slots, f2), BF16),
            pltpu.SemaphoreType.DMA((6 + 2 * (f // 256),)),
        ],
        compiler_params=params(40),
        name="train",
    )(scal, blocks_a, blocks_b, x, gate_up, down)


def turn_kernel(scal, x_a, x_b, out, x, sem):
    slots, wide = x.shape[1:]
    mine = pl.ds(pl.multiple_of(scal[0] * wide, wide), wide)
    loads = [pltpu.make_async_copy(src.at[:, mine], x.at[s], sem.at[s]) for s, src in enumerate((x_a, x_b))]
    for load in loads:
        load.start()
    for s in range(2):
        loads[s].wait()

        def turn(c, _):
            part = pl.ds(pl.multiple_of(c * 256, 256), 256)
            out[part, s * slots:(s + 1) * slots] = x[s, :, part].T
            return 0

        lax.fori_loop(0, wide // 256, turn, 0)


def turned(scal, x_a, x_b):
    slots, d = x_a.shape
    wide = d // 2
    return pl.pallas_call(
        turn_kernel,
        out_shape=jax.ShapeDtypeStruct((wide, 2 * slots), BF16),
        in_specs=[smem(), anywhere(), anywhere()],
        out_specs=vmem(),
        scratch_shapes=[pltpu.VMEM((2, slots, wide), BF16), pltpu.SemaphoreType.DMA((2,))],
        compiler_params=params(12),
        name="turn",
    )(scal, x_a, x_b)


def update_gate_kernel(eta, scal, xt_h, bg_a, bg_b, gu_h, out, x_t, bg, w, stage, sem):
    wide = x_t.shape[0]
    slots = x_t.shape[1] // 2
    groups, four, high, cols = stage.shape[1:]
    steps = stage.shape[0]
    mine = pl.ds(pl.multiple_of(scal[0] * wide, wide), wide)
    load_x = pltpu.make_async_copy(xt_h, x_t, sem.at[0])

    def part(n):
        return pl.ds(pl.multiple_of(n * cols, cols), cols)

    def loads(n):
        return (
            pltpu.make_async_copy(bg_a.at[:, part(n)], bg.at[pl.ds(0, slots), part(n)], sem.at[1 + 3 * n]),
            pltpu.make_async_copy(bg_b.at[:, part(n)], bg.at[pl.ds(slots, slots), part(n)], sem.at[2 + 3 * n]),
            pltpu.make_async_copy(gu_h.at[mine, part(n)], w.at[:, part(n)], sem.at[3 + 3 * n]),
        )

    def save(n):
        rows = pl.ds(pl.multiple_of(n * high, high), high)
        return pltpu.make_async_copy(stage.at[n], out.at[:, :, rows, :], sem.at[1 + 3 * steps + n])

    load_x.start()
    for n in range(steps):
        for load in loads(n):
            load.start()
    load_x.wait()

    def one(n, _):
        for load in loads(n):
            load.wait()
        grad = jnp.dot(x_t[...], bg[:, part(n)], preferred_element_type=F32)
        new = (w[:, part(n)].astype(F32) - eta * grad).astype(BF16)
        stage[n] = new.reshape(groups, four, high, cols)
        save(n).start()
        return 0

    lax.fori_loop(0, steps, one, 0)
    for n in range(steps):
        save(n).wait()


def update_gate(eta, scal, x_t, bg_a, bg_b, gate_up):
    wide, both = x_t.shape
    f2 = bg_a.shape[1]
    high, cols = wide // 64, 256
    steps = f2 // cols
    tall = steps * high + (f2 // 2) // 16
    return pl.pallas_call(
        lambda *refs: update_gate_kernel(eta, *refs),
        out_shape=pltpu.HBM((16, 4, tall, cols), BF16),
        in_specs=[smem()] + [anywhere()] * 4,
        out_specs=anywhere(),
        scratch_shapes=[
            pltpu.VMEM((wide, both), BF16), pltpu.VMEM((both, f2), BF16), pltpu.VMEM((wide, f2), BF16),
            pltpu.VMEM((steps, 16, 4, high, cols), BF16), pltpu.SemaphoreType.DMA((1 + 4 * steps,)),
        ],
        compiler_params=params(32),
        name="update_gate",
    )(scal, x_t, bg_a, bg_b, gate_up)


def update_down_kernel(eta, scal, hid_a, hid_b, og_a, og_b, dw_h, given, out, hid_t, og, w, stage, sem):
    slots = hid_t.shape[1] // 2
    wide = og.shape[1]
    steps, groups, high, cols = stage.shape
    base = out.shape[2] - high
    mine = pl.ds(pl.multiple_of(scal[0] * wide, wide), wide)
    loads = [
        pltpu.make_async_copy(hid_a, hid_t.at[:, pl.ds(0, slots)], sem.at[0]),
        pltpu.make_async_copy(hid_b, hid_t.at[:, pl.ds(slots, slots)], sem.at[1]),
        pltpu.make_async_copy(og_a, og.at[pl.ds(0, slots)], sem.at[2]),
        pltpu.make_async_copy(og_b, og.at[pl.ds(slots, slots)], sem.at[3]),
        pltpu.make_async_copy(dw_h.at[:, mine], w, sem.at[4]),
    ]
    for load in loads:
        load.start()
    for load in loads:
        load.wait()

    def save(n):
        return pltpu.make_async_copy(stage.at[n], out.at[:, n, pl.ds(base, high), :], sem.at[5 + n])

    def one(n, _):
        part = pl.ds(pl.multiple_of(n * cols, cols), cols)
        grad = jnp.dot(hid_t[...], og[:, part], preferred_element_type=F32)
        new = (w[:, part].astype(F32) - eta * grad).astype(BF16)
        stage[n] = new.reshape(groups, high, cols)
        save(n).start()
        return 0

    lax.fori_loop(0, steps, one, 0)
    for n in range(steps):
        save(n).wait()


def update_down(eta, scal, hid_a, hid_b, og_a, og_b, down, given):
    f, slots = hid_a.shape
    wide = og_a.shape[1]
    cols = given.shape[3]
    steps = wide // cols
    high = f // 16
    return pl.pallas_call(
        lambda *refs: update_down_kernel(eta, *refs),
        out_shape=pltpu.HBM(given.shape, BF16),
        in_specs=[smem()] + [anywhere()] * 6,
        out_specs=anywhere(),
        scratch_shapes=[
            pltpu.VMEM((f, 2 * slots), BF16), pltpu.VMEM((2 * slots, wide), BF16), pltpu.VMEM((f, wide), BF16),
            pltpu.VMEM((steps, 16, high, cols), BF16), pltpu.SemaphoreType.DMA((5 + steps,)),
        ],
        input_output_aliases={6: 0},
        compiler_params=params(24),
        name="update_down",
    )(scal, hid_a, hid_b, og_a, og_b, down, given)


def choose_kernel(slot_map, src, out, sem):
    def start(i, _):
        pltpu.make_async_copy(src.at[slot_map[i]], out.at[i], sem).start()
        return 0

    lax.fori_loop(0, out.shape[0], start, 0, unroll=8)
    pltpu.make_async_copy(src, out, sem).wait()


def choose(slot_map, pieces):
    return pl.pallas_call(
        choose_kernel,
        out_shape=jax.ShapeDtypeStruct(pieces.shape, BF16),
        in_specs=[smem(), anywhere()],
        out_specs=vmem(),
        scratch_shapes=[pltpu.SemaphoreType.DMA],
        compiler_params=params(16),
        name="choose",
    )(slot_map, pieces)


def serve_kernel(scal, blocks_a, blocks_b, x_h, w_a, w_b, out, x, gu, dw, hid, sem):
    half = scal[0]
    d = x.shape[1]
    high, f2 = gu.shape[3:]
    f = f2 // 2
    fc, dc = 256, 512
    steps = f2 // fc
    deep = dw.shape[1]
    base = w_a.shape[2] - deep

    load_x = pltpu.make_async_copy(x_h, x, sem.at[0])

    def load_gu(s, n):
        src, place = ((w_a, half), (w_b, 1 - half))[s]
        return pltpu.make_async_copy(
            src.at[:, :, pl.ds(n * high, high), :], gu.at[place, :, :, :, pl.ds(n * fc, fc)], sem.at[1 + 2 * n + s]
        )

    def load_dw(s, n):
        src, place = ((w_a, half), (w_b, 1 - half))[s]
        cols = pl.ds(pl.multiple_of(place * (d // 2) + n * fc, fc), fc)
        return pltpu.make_async_copy(
            src.at[:, n, pl.ds(base, deep), :], dw.at[:, :, cols], sem.at[1 + 2 * steps + 2 * n + s]
        )

    load_x.start()
    for n in range(steps):
        for s in range(2):
            load_gu(s, n).start()
    for n in range(4):
        for s in range(2):
            load_dw(s, n).start()
    load_x.wait()
    kept, scale = kept_and_scale(x[:, :LANES], half, limit_of(1, scal, blocks_a, blocks_b))
    for n in range(steps):
        for s in range(2):
            load_gu(s, n).wait()

    def project(i, _):
        left = pl.ds(pl.multiple_of(i * fc, fc), fc)
        right = pl.ds(pl.multiple_of(f + i * fc, fc), fc)
        g = jnp.dot(x[...], gu[:, :, :, :, left].reshape(d, fc), preferred_element_type=F32)
        u = jnp.dot(x[...], gu[:, :, :, :, right].reshape(d, fc), preferred_element_type=F32)
        hid[:, left] = (g * jax.nn.sigmoid(g) * u).astype(BF16)
        return 0

    lax.fori_loop(0, f // fc, project, 0)
    for n in range(4):
        for s in range(2):
            load_dw(s, n).wait()

    def outputs(c, _):
        cols = pl.ds(pl.multiple_of(c * dc, dc), dc)
        o = jnp.dot(hid[...], dw[:, :, cols].reshape(f, dc), preferred_element_type=F32)
        out[:, cols] = jnp.where(kept, scale * o, 0.0).astype(BF16)
        return 0

    lax.fori_loop(0, d // dc, outputs, 0)


def serve(scal, blocks_a, blocks_b, x, w_a, w_b):
    slots, d = x.shape
    f = d * 3 // 8
    high = d // 2 // 64
    steps = 2 * f // 256
    return pl.pallas_call(
        serve_kernel,
        out_shape=pltpu.HBM((slots, d), BF16),
        in_specs=[smem(), smem(), smem()] + [anywhere()] * 3,
        out_specs=vmem(),
        scratch_shapes=[
            pltpu.VMEM((slots, d), BF16), pltpu.VMEM((2, 16, 4, high, 2 * f), BF16), pltpu.VMEM((16, f // 16, d), BF16),
            pltpu.VMEM((slots, f), BF16), pltpu.SemaphoreType.DMA((9 + 2 * steps,)),
        ],
        compiler_params=params(40),
        name="serve",
    )(scal, blocks_a, blocks_b, x, w_a, w_b)


def unpack_kernel(first, scal, pick, train, serve, given, out, box, done, sem):
    half = scal[0]
    steps = box.shape[0]
    wide = box.shape[2]

    def load(src, c):
        return pltpu.make_async_copy(src.at[:, pl.ds(c * wide, wide)], box.at[c], sem.at[c])

    def save(c):
        return pltpu.make_async_copy(done.at[c], out.at[:, pl.ds(c * wide, wide)], sem.at[steps + c])

    @pl.when(half == 0)
    def _():
        for c in range(steps):
            load(train, c).start()

    @pl.when(half == 1)
    def _():
        for c in range(steps):
            load(serve, c).start()

    for c in range(steps):
        load(train, c).wait()
        rows = jnp.dot(pick[...], box[c], preferred_element_type=F32)
        if not first:
            rows = rows + given[:, c * wide:(c + 1) * wide].astype(F32)
        done[c] = rows.astype(BF16)
        save(c).start()
    for c in range(steps):
        save(c).wait()


def unpack(scal, pick, train, serve, given=None):
    rows, slots = pick.shape
    d = train.shape[1]
    steps = 4
    first = given is None
    return pl.pallas_call(
        lambda *refs: unpack_kernel(first, *refs),
        out_shape=jax.ShapeDtypeStruct((rows, d), BF16),
        in_specs=[smem(), vmem(), anywhere(), anywhere(), smem() if first else vmem()],
        out_specs=anywhere(),
        scratch_shapes=[
            pltpu.VMEM((steps, slots, d // steps), BF16), pltpu.VMEM((steps, rows, d // steps), BF16),
            pltpu.SemaphoreType.DMA((2 * steps,)),
        ],
        compiler_params=params(16),
        name="unpack" if first else "unpack_rest",
    )(scal, pick, train, serve, scal if first else given)


def swap(value):
    return lax.ppermute(value, "half", SWAP)


def spread(value):
    return lax.all_to_all(value, "ep", split_axis=0, concat_axis=0, tiled=True)


def step(activations, routes, blocks, row_scale, gate_up, down_weight, slot_map):
    members = lax.axis_size("ep")
    tokens = activations[0]
    row_count, width = tokens.shape
    boxed = (members, BOX, width)
    flat = (members * BOX, width)
    route = routes.reshape(1, row_count)
    gate_up, down_weight = gate_up[0], down_weight[0]
    scal = jnp.stack([lax.axis_index("half"), lax.axis_index("ep")]).astype(jnp.int32)
    eta = 0.03 / math.sqrt(row_count)

    gate_h, down_h = in_hbm(gate_up, down_weight)
    tokens_b = swap(tokens)
    route_b = swap(route)
    scale_b = swap(row_scale)
    blocks_b = swap(blocks)
    train_p, train_i, serve_p, serve_i, own_p, recv_p = prepare(
        members, scal, *in_hbm(route), route_b, *in_hbm(row_scale), scale_b
    )
    tokens_h = in_hbm(tokens)[0]
    packed = pack(0, scal, tokens_h, tokens_b, train_p, train_i)
    train_rows = spread(packed.reshape(boxed)).reshape(flat)
    packed = pack(1, scal, tokens_h, tokens_b, serve_p, serve_i)
    serve_rows = spread(packed.reshape(boxed)).reshape(flat)

    train_rows_b = swap(train_rows)
    hidden, grad_own, grad_send, both = train(scal, blocks, blocks_b, train_rows, gate_h, down_h)
    both_b = swap(both)
    rows_t = turned(scal, train_rows, train_rows_b)
    hidden_send, grad_send, _ = lax.optimization_barrier((hidden, grad_send, both_b))
    hidden_b = swap(hidden_send)
    grad_b = swap(grad_send)
    new = update_gate(eta, scal, rows_t, both, both_b, gate_h)
    new = update_down(eta, scal, hidden, hidden_b, grad_own, grad_b, down_h, new)
    laid = new.shape
    tiled = (members,) + laid[2:]
    pieces = spread(new.reshape(tiled))
    both, _ = lax.optimization_barrier((both, new))
    input_grad = lax.dot_general(both, gate_up, NT, preferred_element_type=F32).astype(BF16)
    chosen = choose(slot_map, pieces)
    slots = spread(chosen)
    input_grad, _ = lax.optimization_barrier((input_grad, slots))
    train_back = spread(input_grad.reshape(boxed)).reshape(flat)
    slots_b = swap(slots)
    served = serve(scal, blocks, blocks_b, serve_rows, slots.reshape(laid), slots_b.reshape(laid))
    serve_back = spread(served.reshape(boxed)).reshape(flat)
    train_other = swap(train_back)
    serve_other = swap(serve_back)
    rows = unpack(scal, own_p, train_back, serve_back)
    return unpack(scal, recv_p, train_other, serve_other, rows)[None]


def solution(mesh):
    placed = (
        P("half", "ep", None),
        P("half", "ep", None),
        P("half", None),
        P("half", "ep"),
        P("ep", None, None),
        P("ep", None, None),
        P(),
    )
    return jax.shard_map(step, mesh=mesh, in_specs=placed, out_specs=P("half", "ep", None), check_vma=False)
```

```python
import math

import jax
import jax.numpy as jnp
from jax import lax
from jax.experimental import pallas as pl
from jax.experimental.pallas import tpu as pltpu
from jax.sharding import PartitionSpec as P


BLK = 128
PART = 7
BOX = 8
COUNT = 8
LANES = 128
SWAP = [(0, 1), (1, 0)]
F32 = jnp.float32
BF16 = jnp.bfloat16
NT = (((1,), (1,)), ((), ()))


def params(mib=56):
    return pltpu.CompilerParams(vmem_limit_bytes=mib << 20)


def iota(shape, dim):
    return lax.broadcasted_iota(jnp.int32, shape, dim)


def anywhere():
    return pl.BlockSpec(memory_space=pl.ANY)


def in_hbm(*values):
    return [pltpu.with_memory_space_constraint(value, pltpu.HBM) for value in values]


def vmem():
    return pl.BlockSpec(memory_space=pltpu.VMEM)


def smem():
    return pl.BlockSpec(memory_space=pltpu.SMEM)


def order_of(target, members):
    rows = target.shape[1]
    named = iota((members, rows), 0) == target
    onehot = named.astype(BF16)
    upper = (iota((rows, rows), 0) < iota((rows, rows), 1)).astype(BF16)
    before = jnp.dot(onehot, upper, preferred_element_type=F32)
    return jnp.sum(jnp.where(named, before, 0.0), axis=0, keepdims=True).astype(jnp.int32)


def prepare_kernel(members, scal, route_a, route_b, scale_a, scale_b, train_p, train_i, serve_p, serve_i, own_p, recv_p):
    half = scal[0]
    slots = members * BOX
    rows = route_a.shape[1]
    order_a, order_b = order_of(route_a[...], members), order_of(route_b[...], members)
    for group, placer, info in ((0, train_p, train_i), (1, serve_p, serve_i)):
        own = half == group
        target = jnp.where(own, route_a[...], route_b[...])
        scale = jnp.where(own, scale_a[...].astype(F32), scale_b[...].astype(F32))
        order = jnp.where(own, order_a, order_b) - PART * half
        inside = (order >= 0) & (order < PART)
        place = jnp.where(inside, target * BOX + order, -1)
        placer[...] = (iota((slots, rows), 0) == place).astype(BF16)
        tags = (iota((slots, rows), 0) == target * BOX + PART).astype(BF16)
        lane = iota((LANES, rows), 0)
        told = jnp.where((lane == order) & inside, scale, jnp.where(lane == COUNT, 1.0, 0.0)).astype(BF16)
        info[...] = lax.dot_general(tags, told, NT, preferred_element_type=F32).astype(BF16)
    eye = (iota((rows, rows), 0) == iota((rows, rows), 1)).astype(BF16)
    pair = jnp.where(iota((BOX, rows), 0) == 0, route_a[...], order_a).astype(F32).astype(BF16)
    column = lax.dot_general(eye, pair, NT, preferred_element_type=F32).astype(jnp.int32)
    goal, rank = column[:, 0:1], column[:, 1:2]
    for first, pick in ((PART * half, own_p), (PART * (1 - half), recv_p)):
        k = rank - first
        at = jnp.where((k >= 0) & (k < PART), k * members + goal, -1)
        pick[...] = (iota(pick.shape, 1) == at).astype(BF16)


def prepare(members, scal, route_a, route_b, scale_a, scale_b):
    rows = route_a.shape[1]
    slots = members * BOX
    placer = jax.ShapeDtypeStruct((slots, rows), BF16)
    info = jax.ShapeDtypeStruct((slots, LANES), BF16)
    pick = jax.ShapeDtypeStruct((rows, members * PART), BF16)
    return pl.pallas_call(
        lambda *refs: prepare_kernel(members, *refs),
        out_shape=(placer, info, placer, info, pick, pick),
        in_specs=[smem()] + [vmem()] * 4,
        out_specs=(vmem(),) * 6,
        compiler_params=params(16),
        name="prepare",
    )(scal, route_a, route_b, scale_a, scale_b)


def pack_kernel(group, scal, tok_a, tok_b, placer, info, out, tok, packed, sem):
    own = scal[0] == group
    wide = tok.shape[2]
    steps = tok.shape[0]

    def load(src, c):
        return pltpu.make_async_copy(src.at[:, pl.ds(c * wide, wide)], tok.at[c], sem.at[c])

    def save(c):
        return pltpu.make_async_copy(packed.at[c], out.at[:, pl.ds(c * wide, wide)], sem.at[steps + c])

    @pl.when(own)
    def _():
        for c in range(steps):
            load(tok_a, c).start()

    @pl.when(jnp.logical_not(own))
    def _():
        for c in range(steps):
            load(tok_b, c).start()

    for c in range(steps):
        load(tok_a, c).wait()
        box = jnp.dot(placer[...], tok[c], preferred_element_type=F32)
        if c == 0:
            packed[c, :, :LANES] = (box[:, :LANES] + info[...].astype(F32)).astype(BF16)
            packed[c, :, LANES:] = box[:, LANES:].astype(BF16)
        else:
            packed[c] = box.astype(BF16)
        save(c).start()
    for c in range(steps):
        save(c).wait()


def pack(group, scal, tok_a, tok_b, placer, info):
    slots, rows = placer.shape
    width = tok_a.shape[1]
    steps = 4
    return pl.pallas_call(
        lambda *refs: pack_kernel(group, *refs),
        out_shape=pltpu.HBM((slots, width), BF16),
        in_specs=[smem(), anywhere(), anywhere(), vmem(), vmem()],
        out_specs=anywhere(),
        scratch_shapes=[
            pltpu.VMEM((steps, rows, width // steps), BF16), pltpu.VMEM((steps, slots, width // steps), BF16),
            pltpu.SemaphoreType.DMA((2 * steps,)),
        ],
        compiler_params=params(16),
    )(scal, tok_a, tok_b, placer, info)


def kept_and_scale(head, half, limit):
    slots = head.shape[0]
    row = iota((slots, slots), 0) // BOX
    col = iota((slots, slots), 1)
    tag = (col % BOX) == PART
    mine = (tag & (col // BOX == row)).astype(BF16)
    lower = (tag & (col // BOX < row)).astype(BF16)
    here = jnp.dot(mine, head, preferred_element_type=F32)
    below = jnp.dot(lower, head, preferred_element_type=F32)
    lane = iota((slots, LANES), 1)
    place = iota((slots, LANES), 0) % BOX
    scale = jnp.sum(jnp.where(lane == place, here, 0.0), axis=1, keepdims=True)
    total = jnp.sum(jnp.where(lane == COUNT, here, 0.0), axis=1, keepdims=True)
    ahead = jnp.sum(jnp.where(lane == COUNT, below, 0.0), axis=1, keepdims=True)
    k = iota((slots, 1), 0) % BOX
    index = (k + PART * half).astype(F32)
    kept = (k < PART) & (index < total) & (ahead + index < limit.astype(F32))
    return kept, scale


def limit_of(group, scal, blocks_a, blocks_b):
    own = scal[0] == group
    at = scal[1]
    return jnp.where(own, blocks_a[0, at], blocks_b[0, at]) * BLK


def train_kernel(scal, blocks_a, blocks_b, x_h, gu_h, dw_h, hid_h, og_own, og_send, bg_h,
                 x, gu, dw, gate, up, hid, hid_t, og, bg, sem):
    half = scal[0]
    d, f2 = gu.shape
    f = f2 // 2
    fc, dc = 256, 512
    nf, nd = f // fc, d // dc

    def load_gu(i, which):
        cols = pl.ds(pl.multiple_of(which * f + i * fc, fc), fc)
        return pltpu.make_async_copy(gu_h.at[:, cols], gu.at[:, cols], sem.at[2 + 2 * i + which])

    load_x = pltpu.make_async_copy(x_h, x, sem.at[0])
    load_dw = pltpu.make_async_copy(dw_h, dw, sem.at[1])
    load_x.start()
    for i in range(nf):
        load_gu(i, 0).start()
        load_gu(i, 1).start()
    load_dw.start()
    load_x.wait()
    kept, scale = kept_and_scale(x[:, :LANES], half, limit_of(0, scal, blocks_a, blocks_b))
    keep = jnp.where(kept, 1.0, 0.0)

    def project(i, _):
        load_gu(i, 0).wait()
        load_gu(i, 1).wait()
        left = pl.ds(pl.multiple_of(i * fc, fc), fc)
        right = pl.ds(pl.multiple_of(f + i * fc, fc), fc)
        g = jnp.dot(x[...], gu[:, left], preferred_element_type=F32)
        u = jnp.dot(x[...], gu[:, right], preferred_element_type=F32)
        gate[:, left] = g
        up[:, left] = u
        h = (keep * (g * jax.nn.sigmoid(g) * u)).astype(BF16)
        hid[:, left] = h
        hid_t[left, :] = h.T
        return 0

    lax.fori_loop(0, nf, project, 0)
    out_hid = pltpu.make_async_copy(hid_t, hid_h, sem.at[2 + 2 * nf])
    out_hid.start()
    load_dw.wait()

    def outputs(c, _):
        cols = pl.ds(pl.multiple_of(c * dc, dc), dc)
        o = jnp.dot(hid[...], dw[:, cols], preferred_element_type=F32)
        og[:, cols] = (scale * o).astype(BF16)
        return 0

    lax.fori_loop(0, nd, outputs, 0)

    def out_og(which, place):
        cols = pl.ds(pl.multiple_of(place * (d // 2), d // 2), d // 2)
        return pltpu.make_async_copy(og.at[:, cols], (og_own, og_send)[which], sem.at[3 + 2 * nf + which])

    out_og(0, half).start()
    out_og(1, 1 - half).start()

    def hidden_back(i, _):
        left = pl.ds(pl.multiple_of(i * fc, fc), fc)
        right = pl.ds(pl.multiple_of(f + i * fc, fc), fc)
        hg = lax.dot_general(og[...], dw[left, :], NT, preferred_element_type=F32)
        g = gate[:, left]
        s = jax.nn.sigmoid(g)
        bg[:, left] = (hg * up[:, left] * (s * (1.0 + g * (1.0 - s)))).astype(BF16)
        bg[:, right] = (hg * (g * s)).astype(BF16)
        return 0

    lax.fori_loop(0, nf, hidden_back, 0)
    out_bg = pltpu.make_async_copy(bg, bg_h, sem.at[5 + 2 * nf])
    out_bg.start()
    out_hid.wait()
    out_og(0, half).wait()
    out_og(1, 1 - half).wait()
    out_bg.wait()


def train(scal, blocks_a, blocks_b, x, gate_up, down):
    slots, d = x.shape
    f2 = gate_up.shape[1]
    f = f2 // 2
    half_rows = jax.ShapeDtypeStruct((slots, d // 2), BF16)
    return pl.pallas_call(
        train_kernel,
        out_shape=(
            jax.ShapeDtypeStruct((f, slots), BF16), half_rows, half_rows, pltpu.HBM((slots, f2), BF16)
        ),
        in_specs=[smem(), smem(), smem(), anywhere(), anywhere(), anywhere()],
        out_specs=(anywhere(),) * 4,
        scratch_shapes=[
            pltpu.VMEM((slots, d), BF16), pltpu.VMEM((d, f2), BF16), pltpu.VMEM((f, d), BF16),
            pltpu.VMEM((slots, f), F32), pltpu.VMEM((slots, f), F32), pltpu.VMEM((slots, f), BF16),
            pltpu.VMEM((f, slots), BF16), pltpu.VMEM((slots, d), BF16), pltpu.VMEM((slots, f2), BF16),
            pltpu.SemaphoreType.DMA((6 + 2 * (f // 256),)),
        ],
        compiler_params=params(40),
        name="train",
    )(scal, blocks_a, blocks_b, x, gate_up, down)


def turn_kernel(scal, x_a, x_b, out, x, sem):
    slots, wide = x.shape[1:]
    mine = pl.ds(pl.multiple_of(scal[0] * wide, wide), wide)
    loads = [pltpu.make_async_copy(src.at[:, mine], x.at[s], sem.at[s]) for s, src in enumerate((x_a, x_b))]
    for load in loads:
        load.start()
    for s in range(2):
        loads[s].wait()

        def turn(c, _):
            part = pl.ds(pl.multiple_of(c * 256, 256), 256)
            out[part, s * slots:(s + 1) * slots] = x[s, :, part].T
            return 0

        lax.fori_loop(0, wide // 256, turn, 0)


def turned(scal, x_a, x_b):
    slots, d = x_a.shape
    wide = d // 2
    return pl.pallas_call(
        turn_kernel,
        out_shape=jax.ShapeDtypeStruct((wide, 2 * slots), BF16),
        in_specs=[smem(), anywhere(), anywhere()],
        out_specs=vmem(),
        scratch_shapes=[pltpu.VMEM((2, slots, wide), BF16), pltpu.SemaphoreType.DMA((2,))],
        compiler_params=params(12),
        name="turn",
    )(scal, x_a, x_b)


def update_gate_kernel(eta, scal, xt_h, bg_a, bg_b, gu_h, out, x_t, bg, w, stage, sem):
    wide = x_t.shape[0]
    slots = x_t.shape[1] // 2
    groups, four, high, cols = stage.shape[1:]
    steps = stage.shape[0]
    mine = pl.ds(pl.multiple_of(scal[0] * wide, wide), wide)
    load_x = pltpu.make_async_copy(xt_h, x_t, sem.at[0])

    def part(n):
        return pl.ds(pl.multiple_of(n * cols, cols), cols)

    def loads(n):
        return (
            pltpu.make_async_copy(bg_a.at[:, part(n)], bg.at[pl.ds(0, slots), part(n)], sem.at[1 + 3 * n]),
            pltpu.make_async_copy(bg_b.at[:, part(n)], bg.at[pl.ds(slots, slots), part(n)], sem.at[2 + 3 * n]),
            pltpu.make_async_copy(gu_h.at[mine, part(n)], w.at[:, part(n)], sem.at[3 + 3 * n]),
        )

    def save(n):
        rows = pl.ds(pl.multiple_of(n * high, high), high)
        return pltpu.make_async_copy(stage.at[n], out.at[:, :, rows, :], sem.at[1 + 3 * steps + n])

    load_x.start()
    for n in range(steps):
        for load in loads(n):
            load.start()
    load_x.wait()

    def one(n, _):
        for load in loads(n):
            load.wait()
        grad = jnp.dot(x_t[...], bg[:, part(n)], preferred_element_type=F32)
        new = (w[:, part(n)].astype(F32) - eta * grad).astype(BF16)
        stage[n] = new.reshape(groups, four, high, cols)
        save(n).start()
        return 0

    lax.fori_loop(0, steps, one, 0)
    for n in range(steps):
        save(n).wait()


def update_gate(eta, scal, x_t, bg_a, bg_b, gate_up):
    wide, both = x_t.shape
    f2 = bg_a.shape[1]
    high, cols = wide // 64, 256
    steps = f2 // cols
    tall = steps * high + (f2 // 2) // 16
    return pl.pallas_call(
        lambda *refs: update_gate_kernel(eta, *refs),
        out_shape=pltpu.HBM((16, 4, tall, cols), BF16),
        in_specs=[smem()] + [anywhere()] * 4,
        out_specs=anywhere(),
        scratch_shapes=[
            pltpu.VMEM((wide, both), BF16), pltpu.VMEM((both, f2), BF16), pltpu.VMEM((wide, f2), BF16),
            pltpu.VMEM((steps, 16, 4, high, cols), BF16), pltpu.SemaphoreType.DMA((1 + 4 * steps,)),
        ],
        compiler_params=params(32),
        name="update_gate",
    )(scal, x_t, bg_a, bg_b, gate_up)


def update_down_kernel(eta, scal, hid_a, hid_b, og_a, og_b, dw_h, given, out, hid_t, og, w, stage, sem):
    slots = hid_t.shape[1] // 2
    wide = og.shape[1]
    steps, groups, high, cols = stage.shape
    base = out.shape[2] - high
    first = [
        pltpu.make_async_copy(hid_a, hid_t.at[:, pl.ds(0, slots)], sem.at[0]),
        pltpu.make_async_copy(hid_b, hid_t.at[:, pl.ds(slots, slots)], sem.at[1]),
    ]

    def part(n):
        return pl.ds(pl.multiple_of(n * cols, cols), cols)

    def loads(n):
        theirs = pl.ds(pl.multiple_of(scal[0] * wide + n * cols, cols), cols)
        return (
            pltpu.make_async_copy(og_a.at[:, part(n)], og.at[pl.ds(0, slots), part(n)], sem.at[2 + 3 * n]),
            pltpu.make_async_copy(og_b.at[:, part(n)], og.at[pl.ds(slots, slots), part(n)], sem.at[3 + 3 * n]),
            pltpu.make_async_copy(dw_h.at[:, theirs], w.at[:, part(n)], sem.at[4 + 3 * n]),
        )

    for load in first:
        load.start()
    for n in range(steps):
        for load in loads(n):
            load.start()
    for load in first:
        load.wait()

    def save(n):
        return pltpu.make_async_copy(stage.at[n], out.at[:, n, pl.ds(base, high), :], sem.at[2 + 3 * steps + n])

    def one(n, _):
        for load in loads(n):
            load.wait()
        grad = jnp.dot(hid_t[...], og[:, part(n)], preferred_element_type=F32)
        new = (w[:, part(n)].astype(F32) - eta * grad).astype(BF16)
        stage[n] = new.reshape(groups, high, cols)
        save(n).start()
        return 0

    lax.fori_loop(0, steps, one, 0)
    for n in range(steps):
        save(n).wait()


def update_down(eta, scal, hid_a, hid_b, og_a, og_b, down, given):
    f, slots = hid_a.shape
    wide = og_a.shape[1]
    cols = given.shape[3]
    steps = wide // cols
    high = f // 16
    return pl.pallas_call(
        lambda *refs: update_down_kernel(eta, *refs),
        out_shape=pltpu.HBM(given.shape, BF16),
        in_specs=[smem()] + [anywhere()] * 6,
        out_specs=anywhere(),
        scratch_shapes=[
            pltpu.VMEM((f, 2 * slots), BF16), pltpu.VMEM((2 * slots, wide), BF16), pltpu.VMEM((f, wide), BF16),
            pltpu.VMEM((steps, 16, high, cols), BF16), pltpu.SemaphoreType.DMA((2 + 4 * steps,)),
        ],
        input_output_aliases={6: 0},
        compiler_params=params(24),
        name="update_down",
    )(scal, hid_a, hid_b, og_a, og_b, down, given)


def choose_kernel(slot_map, src, out, sem):
    def start(i, _):
        pltpu.make_async_copy(src.at[slot_map[i]], out.at[i], sem).start()
        return 0

    lax.fori_loop(0, out.shape[0], start, 0, unroll=8)
    pltpu.make_async_copy(src, out, sem).wait()


def choose(slot_map, pieces):
    return pl.pallas_call(
        choose_kernel,
        out_shape=jax.ShapeDtypeStruct(pieces.shape, BF16),
        in_specs=[smem(), anywhere()],
        out_specs=vmem(),
        scratch_shapes=[pltpu.SemaphoreType.DMA],
        compiler_params=params(16),
        name="choose",
    )(slot_map, pieces)


def fold(rows, chunk, c, boxed):
    tiles = chunk.shape[0]
    members = rows.shape[0] // BOX
    for i in range(tiles):
        chunk[i] = rows[:, i * LANES:(i + 1) * LANES]
        for k in range(PART):
            boxed[k * tiles + i, pl.ds(c, members, stride=BOX), :] = chunk[i, pl.ds(k, members, stride=BOX), :]


def rounded(boxed, out):
    for i in range(boxed.shape[0]):
        out[:, i * LANES:(i + 1) * LANES] = boxed[i].astype(BF16)


def back_kernel(bg_h, gu_h, out, bg, gu, chunk, boxed, done, sem):
    steps, wide = gu.shape[:2]
    load_bg = pltpu.make_async_copy(bg_h, bg, sem.at[0])

    def load(c):
        return pltpu.make_async_copy(gu_h.at[pl.ds(pl.multiple_of(c * wide, wide), wide)], gu.at[c], sem.at[1 + c])

    load_bg.start()
    for c in range(steps):
        load(c).start()
    load_bg.wait()

    def one(c, _):
        load(c).wait()
        fold(lax.dot_general(bg[...], gu[c], NT, preferred_element_type=F32), chunk, c, boxed)
        return 0

    lax.fori_loop(0, steps, one, 0)
    rounded(boxed, done)
    save = pltpu.make_async_copy(done, out, sem.at[1 + steps])
    save.start()
    save.wait()


def folded(members, d):
    wide = d // BOX
    return [
        pltpu.VMEM((wide // LANES, members * BOX, LANES), F32),
        pltpu.VMEM((PART * wide // LANES, members * BOX, LANES), F32),
    ]


def back(members, bg, gate_up):
    slots, f2 = bg.shape
    d = gate_up.shape[0]
    wide = d // BOX
    shape = (members * BOX, PART * wide)
    return pl.pallas_call(
        back_kernel,
        out_shape=pltpu.HBM(shape, BF16),
        in_specs=[anywhere()] * 2,
        out_specs=anywhere(),
        scratch_shapes=[pltpu.VMEM((slots, f2), BF16), pltpu.VMEM((BOX, wide, f2), BF16)] + folded(members, d) + [
            pltpu.VMEM(shape, BF16), pltpu.SemaphoreType.DMA((2 + BOX,)),
        ],
        compiler_params=params(32),
        name="back",
    )(bg, gate_up)


def serve_kernel(scal, blocks_a, blocks_b, x_h, w_a, w_b, out, x, gu, dw, hid, chunk, boxed, sem):
    half = scal[0]
    d = x.shape[1]
    high, f2 = gu.shape[3:]
    f = f2 // 2
    fc = 256
    steps = f2 // fc
    deep = dw.shape[1]
    base = w_a.shape[2] - deep

    load_x = pltpu.make_async_copy(x_h, x, sem.at[0])

    def load_gu(s, n):
        src, place = ((w_a, half), (w_b, 1 - half))[s]
        return pltpu.make_async_copy(
            src.at[:, :, pl.ds(n * high, high), :], gu.at[place, :, :, :, pl.ds(n * fc, fc)], sem.at[1 + 2 * n + s]
        )

    def load_dw(s, n):
        src, place = ((w_a, half), (w_b, 1 - half))[s]
        cols = pl.ds(pl.multiple_of(place * (d // 2) + n * fc, fc), fc)
        return pltpu.make_async_copy(
            src.at[:, n, pl.ds(base, deep), :], dw.at[:, :, cols], sem.at[1 + 2 * steps + 2 * n + s]
        )

    load_x.start()
    for n in range(steps):
        for s in range(2):
            load_gu(s, n).start()
    for n in range(4):
        for s in range(2):
            load_dw(s, n).start()
    load_x.wait()
    kept, scale = kept_and_scale(x[:, :LANES], half, limit_of(1, scal, blocks_a, blocks_b))
    for n in range(steps):
        for s in range(2):
            load_gu(s, n).wait()

    def project(i, _):
        left = pl.ds(pl.multiple_of(i * fc, fc), fc)
        right = pl.ds(pl.multiple_of(f + i * fc, fc), fc)
        g = jnp.dot(x[...], gu[:, :, :, :, left].reshape(d, fc), preferred_element_type=F32)
        u = jnp.dot(x[...], gu[:, :, :, :, right].reshape(d, fc), preferred_element_type=F32)
        hid[:, left] = (g * jax.nn.sigmoid(g) * u).astype(BF16)
        return 0

    lax.fori_loop(0, f // fc, project, 0)
    for n in range(4):
        for s in range(2):
            load_dw(s, n).wait()

    wide = d // BOX

    def outputs(c, _):
        cols = pl.ds(pl.multiple_of(c * wide, wide), wide)
        o = jnp.dot(hid[...], dw[:, :, cols].reshape(f, wide), preferred_element_type=F32)
        fold(jnp.where(kept, scale * o, 0.0), chunk, c, boxed)
        return 0

    lax.fori_loop(0, BOX, outputs, 0)
    rounded(boxed, out)


def serve(members, scal, blocks_a, blocks_b, x, w_a, w_b):
    slots, d = x.shape
    f = d * 3 // 8
    high = d // 2 // 64
    steps = 2 * f // 256
    return pl.pallas_call(
        serve_kernel,
        out_shape=pltpu.HBM((members * BOX, PART * d // BOX), BF16),
        in_specs=[smem(), smem(), smem()] + [anywhere()] * 3,
        out_specs=vmem(),
        scratch_shapes=[
            pltpu.VMEM((slots, d), BF16), pltpu.VMEM((2, 16, 4, high, 2 * f), BF16), pltpu.VMEM((16, f // 16, d), BF16),
            pltpu.VMEM((slots, f), BF16), *folded(members, d), pltpu.SemaphoreType.DMA((9 + 2 * steps,)),
        ],
        compiler_params=params(40),
        name="serve",
    )(scal, blocks_a, blocks_b, x, w_a, w_b)


def unpack_kernel(first, scal, pick, train, serve, given, out, box, wide_box, rows, done, sem):
    half = scal[0]
    parts = 4
    high = box.shape[0] // parts
    wide = box.shape[1] // PART
    members = box.shape[0] // BOX
    tiles = wide // LANES

    def load(src, i):
        part = pl.ds(i * high, high)
        return pltpu.make_async_copy(src.at[part], box.at[part], sem.at[i])

    def save(c):
        cols = pl.ds(pl.multiple_of(c * wide, wide), wide)
        return pltpu.make_async_copy(done.at[:, cols], out.at[:, cols], sem.at[parts + c])

    @pl.when(half == 0)
    def _():
        for i in range(parts):
            load(train, i).start()

    @pl.when(half == 1)
    def _():
        for i in range(parts):
            load(serve, i).start()

    for i in range(parts):
        load(train, i).wait()
        part = slice(i * high, (i + 1) * high)
        for j in range(wide_box.shape[0]):
            wide_box[j, part, :] = box[part, j * LANES:(j + 1) * LANES].astype(F32)

    def one(c, _):
        cols = pl.ds(pl.multiple_of(c * wide, wide), wide)
        for k in range(PART):
            for i in range(tiles):
                rows[k * members:(k + 1) * members, i * LANES:(i + 1) * LANES] = wide_box[
                    k * tiles + i, pl.ds(c, members, stride=BOX), :
                ].astype(BF16)
        total = jnp.dot(pick[...], rows[...], preferred_element_type=F32)
        if not first:
            total = total + given[:, cols].astype(F32)
        done[:, cols] = total.astype(BF16)
        save(c).start()
        return 0

    lax.fori_loop(0, BOX, one, 0)
    for c in range(BOX):
        save(c).wait()


def unpack(scal, pick, train, serve, given=None):
    rows, slots = pick.shape
    wide = train.shape[1] // PART
    d = wide * BOX
    first = given is None
    return pl.pallas_call(
        lambda *refs: unpack_kernel(first, *refs),
        out_shape=jax.ShapeDtypeStruct((rows, d), BF16),
        in_specs=[smem(), vmem(), anywhere(), anywhere(), smem() if first else vmem()],
        out_specs=anywhere(),
        scratch_shapes=[
            pltpu.VMEM(train.shape, BF16), pltpu.VMEM((train.shape[1] // LANES, train.shape[0], LANES), F32),
            pltpu.VMEM((slots, wide), BF16),
            pltpu.VMEM((rows, d), BF16), pltpu.SemaphoreType.DMA((4 + BOX,)),
        ],
        compiler_params=params(16),
        name="unpack" if first else "unpack_rest",
    )(scal, pick, train, serve, scal if first else given)


def swap(value):
    return lax.ppermute(value, "half", SWAP)


def spread(value):
    return lax.all_to_all(value, "ep", split_axis=0, concat_axis=0, tiled=True)


def step(activations, routes, blocks, row_scale, gate_up, down_weight, slot_map):
    members = lax.axis_size("ep")
    tokens = activations[0]
    row_count, width = tokens.shape
    boxed = (members, BOX, width)
    flat = (members * BOX, width)
    route = routes.reshape(1, row_count)
    gate_up, down_weight = gate_up[0], down_weight[0]
    scal = jnp.stack([lax.axis_index("half"), lax.axis_index("ep")]).astype(jnp.int32)
    eta = 0.03 / math.sqrt(row_count)

    gate_h, down_h = in_hbm(gate_up, down_weight)
    tokens_b = swap(tokens)
    route_b = swap(route)
    scale_b = swap(row_scale)
    blocks_b = swap(blocks)
    train_p, train_i, serve_p, serve_i, own_p, recv_p = prepare(
        members, scal, *in_hbm(route), route_b, *in_hbm(row_scale), scale_b
    )
    tokens_h = in_hbm(tokens)[0]
    packed = pack(0, scal, tokens_h, tokens_b, train_p, train_i)
    train_rows = spread(packed.reshape(boxed)).reshape(flat)
    packed = pack(1, scal, tokens_h, tokens_b, serve_p, serve_i)
    serve_rows = spread(packed.reshape(boxed)).reshape(flat)

    train_rows_b = swap(train_rows)
    hidden, grad_own, grad_send, both = train(scal, blocks, blocks_b, train_rows, gate_h, down_h)
    both_b = swap(both)
    rows_t = turned(scal, train_rows, train_rows_b)
    hidden_send, grad_send, _ = lax.optimization_barrier((hidden, grad_send, both_b))
    hidden_b = swap(hidden_send)
    grad_b = swap(grad_send)
    new = update_gate(eta, scal, rows_t, both, both_b, gate_h)
    new = update_down(eta, scal, hidden, hidden_b, grad_own, grad_b, down_h, new)
    laid = new.shape
    tiled = (members,) + laid[2:]
    pieces = spread(new.reshape(tiled))
    both, _ = lax.optimization_barrier((both, new))
    input_grad = back(members, both, gate_h)
    chosen = choose(slot_map, pieces)
    slots = spread(chosen)
    input_grad, _ = lax.optimization_barrier((input_grad, slots))
    train_back = spread(input_grad.reshape((members, BOX, -1))).reshape(input_grad.shape)
    slots_b = swap(slots)
    served = serve(members, scal, blocks, blocks_b, serve_rows, slots.reshape(laid), slots_b.reshape(laid))
    serve_back = spread(served.reshape((members, BOX, -1))).reshape(served.shape)
    train_other = swap(train_back)
    serve_other = swap(serve_back)
    rows = unpack(scal, own_p, train_back, serve_back)
    return unpack(scal, recv_p, train_other, serve_other, rows)[None]


def solution(mesh):
    placed = (
        P("half", "ep", None),
        P("half", "ep", None),
        P("half", None),
        P("half", "ep"),
        P("ep", None, None),
        P("ep", None, None),
        P(),
    )
    return jax.shard_map(step, mesh=mesh, in_specs=placed, out_specs=P("half", "ep", None), check_vma=False)
```

```python
import math

import jax
import jax.numpy as jnp
from jax import lax
from jax.experimental import pallas as pl
from jax.experimental.pallas import tpu as pltpu
from jax.sharding import PartitionSpec as P


BLK = 128
PART = 7
BOX = 8
COUNT = 8
LANES = 128
SWAP = [(0, 1), (1, 0)]
F32 = jnp.float32
BF16 = jnp.bfloat16
NT = (((1,), (1,)), ((), ()))


def params(mib=56):
    return pltpu.CompilerParams(vmem_limit_bytes=mib << 20)


def iota(shape, dim):
    return lax.broadcasted_iota(jnp.int32, shape, dim)


def anywhere():
    return pl.BlockSpec(memory_space=pl.ANY)


def in_hbm(*values):
    return [pltpu.with_memory_space_constraint(value, pltpu.HBM) for value in values]


def vmem():
    return pl.BlockSpec(memory_space=pltpu.VMEM)


def smem():
    return pl.BlockSpec(memory_space=pltpu.SMEM)


def order_of(target, members):
    rows = target.shape[1]
    named = iota((members, rows), 0) == target
    onehot = named.astype(BF16)
    upper = (iota((rows, rows), 0) < iota((rows, rows), 1)).astype(BF16)
    before = jnp.dot(onehot, upper, preferred_element_type=F32)
    return jnp.sum(jnp.where(named, before, 0.0), axis=0, keepdims=True).astype(jnp.int32)


def prepare_kernel(members, scal, route_a, route_b, scale_a, scale_b, train_p, train_i, serve_p, serve_i, own_p, recv_p):
    half = scal[0]
    slots = members * BOX
    rows = route_a.shape[1]
    order_a, order_b = order_of(route_a[...], members), order_of(route_b[...], members)
    for group, placer, info in ((0, train_p, train_i), (1, serve_p, serve_i)):
        own = half == group
        target = jnp.where(own, route_a[...], route_b[...])
        scale = jnp.where(own, scale_a[...].astype(F32), scale_b[...].astype(F32))
        order = jnp.where(own, order_a, order_b) - PART * half
        inside = (order >= 0) & (order < PART)
        place = jnp.where(inside, target * BOX + order, -1)
        placer[...] = (iota((slots, rows), 0) == place).astype(BF16)
        tags = (iota((slots, rows), 0) == target * BOX + PART).astype(BF16)
        lane = iota((LANES, rows), 0)
        told = jnp.where((lane == order) & inside, scale, jnp.where(lane == COUNT, 1.0, 0.0)).astype(BF16)
        info[...] = lax.dot_general(tags, told, NT, preferred_element_type=F32).astype(BF16)
    eye = (iota((rows, rows), 0) == iota((rows, rows), 1)).astype(BF16)
    pair = jnp.where(iota((BOX, rows), 0) == 0, route_a[...], order_a).astype(F32).astype(BF16)
    column = lax.dot_general(eye, pair, NT, preferred_element_type=F32).astype(jnp.int32)
    goal, rank = column[:, 0:1], column[:, 1:2]
    for first, pick in ((PART * half, own_p), (PART * (1 - half), recv_p)):
        k = rank - first
        at = jnp.where((k >= 0) & (k < PART), k * members + goal, -1)
        pick[...] = (iota(pick.shape, 1) == at).astype(BF16)


def prepare(members, scal, route_a, route_b, scale_a, scale_b):
    rows = route_a.shape[1]
    slots = members * BOX
    placer = jax.ShapeDtypeStruct((slots, rows), BF16)
    info = jax.ShapeDtypeStruct((slots, LANES), BF16)
    pick = jax.ShapeDtypeStruct((rows, members * PART), BF16)
    return pl.pallas_call(
        lambda *refs: prepare_kernel(members, *refs),
        out_shape=(placer, info, placer, info, pick, pick),
        in_specs=[smem()] + [vmem()] * 4,
        out_specs=(vmem(),) * 6,
        compiler_params=params(16),
        name="prepare",
    )(scal, route_a, route_b, scale_a, scale_b)


def pack_kernel(group, scal, tok_a, tok_b, placer, info, out, tok, packed, sem):
    own = scal[0] == group
    wide = tok.shape[2]
    steps = tok.shape[0]

    def load(src, c):
        return pltpu.make_async_copy(src.at[:, pl.ds(c * wide, wide)], tok.at[c], sem.at[c])

    def save(c):
        return pltpu.make_async_copy(packed.at[c], out.at[:, pl.ds(c * wide, wide)], sem.at[steps + c])

    @pl.when(own)
    def _():
        for c in range(steps):
            load(tok_a, c).start()

    @pl.when(jnp.logical_not(own))
    def _():
        for c in range(steps):
            load(tok_b, c).start()

    for c in range(steps):
        load(tok_a, c).wait()
        box = jnp.dot(placer[...], tok[c], preferred_element_type=F32)
        if c == 0:
            packed[c, :, :LANES] = (box[:, :LANES] + info[...].astype(F32)).astype(BF16)
            packed[c, :, LANES:] = box[:, LANES:].astype(BF16)
        else:
            packed[c] = box.astype(BF16)
        save(c).start()
    for c in range(steps):
        save(c).wait()


def pack(group, scal, tok_a, tok_b, placer, info):
    slots, rows = placer.shape
    width = tok_a.shape[1]
    steps = 2
    return pl.pallas_call(
        lambda *refs: pack_kernel(group, *refs),
        out_shape=pltpu.HBM((slots, width), BF16),
        in_specs=[smem(), anywhere(), anywhere(), vmem(), vmem()],
        out_specs=anywhere(),
        scratch_shapes=[
            pltpu.VMEM((steps, rows, width // steps), BF16), pltpu.VMEM((steps, slots, width // steps), BF16),
            pltpu.SemaphoreType.DMA((2 * steps,)),
        ],
        compiler_params=params(16),
    )(scal, tok_a, tok_b, placer, info)


def kept_and_scale(head, half, limit):
    slots = head.shape[0]
    row = iota((slots, slots), 0) // BOX
    col = iota((slots, slots), 1)
    tag = (col % BOX) == PART
    mine = (tag & (col // BOX == row)).astype(BF16)
    lower = (tag & (col // BOX < row)).astype(BF16)
    here = jnp.dot(mine, head, preferred_element_type=F32)
    below = jnp.dot(lower, head, preferred_element_type=F32)
    lane = iota((slots, LANES), 1)
    place = iota((slots, LANES), 0) % BOX
    scale = jnp.sum(jnp.where(lane == place, here, 0.0), axis=1, keepdims=True)
    total = jnp.sum(jnp.where(lane == COUNT, here, 0.0), axis=1, keepdims=True)
    ahead = jnp.sum(jnp.where(lane == COUNT, below, 0.0), axis=1, keepdims=True)
    k = iota((slots, 1), 0) % BOX
    index = (k + PART * half).astype(F32)
    kept = (k < PART) & (index < total) & (ahead + index < limit.astype(F32))
    return kept, scale


def limit_of(group, scal, blocks_a, blocks_b):
    own = scal[0] == group
    at = scal[1]
    return jnp.where(own, blocks_a[0, at], blocks_b[0, at]) * BLK


def train_kernel(scal, blocks_a, blocks_b, x_h, gu_h, dw_h, hid_h, og_own, og_send, bg_h,
                 x, gu, dw, gate, up, hid, hid_t, og, bg, sem):
    half = scal[0]
    d, f2 = gu.shape
    f = f2 // 2
    fc, dc = 256, 512
    nf, nd = f // fc, d // dc

    def load_gu(i, which):
        cols = pl.ds(pl.multiple_of(which * f + i * fc, fc), fc)
        return pltpu.make_async_copy(gu_h.at[:, cols], gu.at[:, cols], sem.at[2 + 2 * i + which])

    load_x = pltpu.make_async_copy(x_h, x, sem.at[0])
    load_dw = pltpu.make_async_copy(dw_h, dw, sem.at[1])
    load_x.start()
    for i in range(nf):
        load_gu(i, 0).start()
        load_gu(i, 1).start()
    load_dw.start()
    load_x.wait()
    kept, scale = kept_and_scale(x[:, :LANES], half, limit_of(0, scal, blocks_a, blocks_b))
    keep = jnp.where(kept, 1.0, 0.0)

    def project(i, _):
        load_gu(i, 0).wait()
        load_gu(i, 1).wait()
        left = pl.ds(pl.multiple_of(i * fc, fc), fc)
        right = pl.ds(pl.multiple_of(f + i * fc, fc), fc)
        g = jnp.dot(x[...], gu[:, left], preferred_element_type=F32)
        u = jnp.dot(x[...], gu[:, right], preferred_element_type=F32)
        gate[:, left] = g
        up[:, left] = u
        h = (keep * (g * jax.nn.sigmoid(g) * u)).astype(BF16)
        hid[:, left] = h
        hid_t[left, :] = h.T
        return 0

    lax.fori_loop(0, nf, project, 0)
    out_hid = pltpu.make_async_copy(hid_t, hid_h, sem.at[2 + 2 * nf])
    out_hid.start()
    load_dw.wait()

    def outputs(c, _):
        cols = pl.ds(pl.multiple_of(c * dc, dc), dc)
        o = jnp.dot(hid[...], dw[:, cols], preferred_element_type=F32)
        og[:, cols] = (scale * o).astype(BF16)
        return 0

    lax.fori_loop(0, nd, outputs, 0)

    def out_og(which, place):
        cols = pl.ds(pl.multiple_of(place * (d // 2), d // 2), d // 2)
        return pltpu.make_async_copy(og.at[:, cols], (og_own, og_send)[which], sem.at[3 + 2 * nf + which])

    out_og(0, half).start()
    out_og(1, 1 - half).start()

    def hidden_back(i, _):
        left = pl.ds(pl.multiple_of(i * fc, fc), fc)
        right = pl.ds(pl.multiple_of(f + i * fc, fc), fc)
        hg = lax.dot_general(og[...], dw[left, :], NT, preferred_element_type=F32)
        g = gate[:, left]
        s = jax.nn.sigmoid(g)
        bg[:, left] = (hg * up[:, left] * (s * (1.0 + g * (1.0 - s)))).astype(BF16)
        bg[:, right] = (hg * (g * s)).astype(BF16)
        return 0

    lax.fori_loop(0, nf, hidden_back, 0)
    out_bg = pltpu.make_async_copy(bg, bg_h, sem.at[5 + 2 * nf])
    out_bg.start()
    out_hid.wait()
    out_og(0, half).wait()
    out_og(1, 1 - half).wait()
    out_bg.wait()


def train(scal, blocks_a, blocks_b, x, gate_up, down):
    slots, d = x.shape
    f2 = gate_up.shape[1]
    f = f2 // 2
    half_rows = jax.ShapeDtypeStruct((slots, d // 2), BF16)
    return pl.pallas_call(
        train_kernel,
        out_shape=(
            jax.ShapeDtypeStruct((f, slots), BF16), half_rows, half_rows, pltpu.HBM((slots, f2), BF16)
        ),
        in_specs=[smem(), smem(), smem(), anywhere(), anywhere(), anywhere()],
        out_specs=(anywhere(),) * 4,
        scratch_shapes=[
            pltpu.VMEM((slots, d), BF16), pltpu.VMEM((d, f2), BF16), pltpu.VMEM((f, d), BF16),
            pltpu.VMEM((slots, f), F32), pltpu.VMEM((slots, f), F32), pltpu.VMEM((slots, f), BF16),
            pltpu.VMEM((f, slots), BF16), pltpu.VMEM((slots, d), BF16), pltpu.VMEM((slots, f2), BF16),
            pltpu.SemaphoreType.DMA((6 + 2 * (f // 256),)),
        ],
        compiler_params=params(40),
        name="train",
    )(scal, blocks_a, blocks_b, x, gate_up, down)


def turn_kernel(scal, x_a, x_b, out, x, sem):
    slots, wide = x.shape[1:]
    mine = pl.ds(pl.multiple_of(scal[0] * wide, wide), wide)
    loads = [pltpu.make_async_copy(src.at[:, mine], x.at[s], sem.at[s]) for s, src in enumerate((x_a, x_b))]
    for load in loads:
        load.start()
    for s in range(2):
        loads[s].wait()

        def turn(c, _):
            part = pl.ds(pl.multiple_of(c * 256, 256), 256)
            out[part, s * slots:(s + 1) * slots] = x[s, :, part].T
            return 0

        lax.fori_loop(0, wide // 256, turn, 0)


def turned(scal, x_a, x_b):
    slots, d = x_a.shape
    wide = d // 2
    return pl.pallas_call(
        turn_kernel,
        out_shape=jax.ShapeDtypeStruct((wide, 2 * slots), BF16),
        in_specs=[smem(), anywhere(), anywhere()],
        out_specs=vmem(),
        scratch_shapes=[pltpu.VMEM((2, slots, wide), BF16), pltpu.SemaphoreType.DMA((2,))],
        compiler_params=params(12),
        name="turn",
    )(scal, x_a, x_b)


def update_gate_kernel(eta, scal, xt_h, bg_a, bg_b, gu_h, out, x_t, bg, w, stage, sem):
    wide = x_t.shape[0]
    slots = x_t.shape[1] // 2
    groups, four, high, cols = stage.shape[1:]
    steps = stage.shape[0]
    mine = pl.ds(pl.multiple_of(scal[0] * wide, wide), wide)
    load_x = pltpu.make_async_copy(xt_h, x_t, sem.at[0])

    def part(n):
        return pl.ds(pl.multiple_of(n * cols, cols), cols)

    def loads(n):
        return (
            pltpu.make_async_copy(bg_a.at[:, part(n)], bg.at[pl.ds(0, slots), part(n)], sem.at[1 + 3 * n]),
            pltpu.make_async_copy(bg_b.at[:, part(n)], bg.at[pl.ds(slots, slots), part(n)], sem.at[2 + 3 * n]),
            pltpu.make_async_copy(gu_h.at[mine, part(n)], w.at[:, part(n)], sem.at[3 + 3 * n]),
        )

    def save(n):
        rows = pl.ds(pl.multiple_of(n * high, high), high)
        return pltpu.make_async_copy(stage.at[n], out.at[:, :, rows, :], sem.at[1 + 3 * steps + n])

    load_x.start()
    for n in range(steps):
        for load in loads(n):
            load.start()
    load_x.wait()

    def one(n, _):
        for load in loads(n):
            load.wait()
        grad = jnp.dot(x_t[...], bg[:, part(n)], preferred_element_type=F32)
        new = (w[:, part(n)].astype(F32) - eta * grad).astype(BF16)
        stage[n] = new.reshape(groups, four, high, cols)
        save(n).start()
        return 0

    lax.fori_loop(0, steps, one, 0)
    for n in range(steps):
        save(n).wait()


def update_gate(eta, scal, x_t, bg_a, bg_b, gate_up):
    wide, both = x_t.shape
    f2 = bg_a.shape[1]
    high, cols = wide // 64, 256
    steps = f2 // cols
    tall = steps * high + (f2 // 2) // 16
    return pl.pallas_call(
        lambda *refs: update_gate_kernel(eta, *refs),
        out_shape=pltpu.HBM((16, 4, tall, cols), BF16),
        in_specs=[smem()] + [anywhere()] * 4,
        out_specs=anywhere(),
        scratch_shapes=[
            pltpu.VMEM((wide, both), BF16), pltpu.VMEM((both, f2), BF16), pltpu.VMEM((wide, f2), BF16),
            pltpu.VMEM((steps, 16, 4, high, cols), BF16), pltpu.SemaphoreType.DMA((1 + 4 * steps,)),
        ],
        compiler_params=params(32),
        name="update_gate",
    )(scal, x_t, bg_a, bg_b, gate_up)


def update_down_kernel(eta, scal, hid_a, hid_b, og_a, og_b, dw_h, given, out, hid_t, og, w, stage, sem):
    slots = hid_t.shape[1] // 2
    wide = og.shape[1]
    steps, groups, high, cols = stage.shape
    base = out.shape[2] - high
    first = [
        pltpu.make_async_copy(hid_a, hid_t.at[:, pl.ds(0, slots)], sem.at[0]),
        pltpu.make_async_copy(hid_b, hid_t.at[:, pl.ds(slots, slots)], sem.at[1]),
    ]

    def part(n):
        return pl.ds(pl.multiple_of(n * cols, cols), cols)

    def loads(n):
        theirs = pl.ds(pl.multiple_of(scal[0] * wide + n * cols, cols), cols)
        return (
            pltpu.make_async_copy(og_a.at[:, part(n)], og.at[pl.ds(0, slots), part(n)], sem.at[2 + 3 * n]),
            pltpu.make_async_copy(og_b.at[:, part(n)], og.at[pl.ds(slots, slots), part(n)], sem.at[3 + 3 * n]),
            pltpu.make_async_copy(dw_h.at[:, theirs], w.at[:, part(n)], sem.at[4 + 3 * n]),
        )

    for load in first:
        load.start()
    for n in range(steps):
        for load in loads(n):
            load.start()
    for load in first:
        load.wait()

    def save(n):
        return pltpu.make_async_copy(stage.at[n], out.at[:, n, pl.ds(base, high), :], sem.at[2 + 3 * steps + n])

    def one(n, _):
        for load in loads(n):
            load.wait()
        grad = jnp.dot(hid_t[...], og[:, part(n)], preferred_element_type=F32)
        new = (w[:, part(n)].astype(F32) - eta * grad).astype(BF16)
        stage[n] = new.reshape(groups, high, cols)
        save(n).start()
        return 0

    lax.fori_loop(0, steps, one, 0)
    for n in range(steps):
        save(n).wait()


def update_down(eta, scal, hid_a, hid_b, og_a, og_b, down, given):
    f, slots = hid_a.shape
    wide = og_a.shape[1]
    cols = given.shape[3]
    steps = wide // cols
    high = f // 16
    return pl.pallas_call(
        lambda *refs: update_down_kernel(eta, *refs),
        out_shape=pltpu.HBM(given.shape, BF16),
        in_specs=[smem()] + [anywhere()] * 6,
        out_specs=anywhere(),
        scratch_shapes=[
            pltpu.VMEM((f, 2 * slots), BF16), pltpu.VMEM((2 * slots, wide), BF16), pltpu.VMEM((f, wide), BF16),
            pltpu.VMEM((steps, 16, high, cols), BF16), pltpu.SemaphoreType.DMA((2 + 4 * steps,)),
        ],
        input_output_aliases={6: 0},
        compiler_params=params(24),
        name="update_down",
    )(scal, hid_a, hid_b, og_a, og_b, down, given)


def choose_kernel(slot_map, src, out, sem):
    def start(i, _):
        pltpu.make_async_copy(src.at[slot_map[i]], out.at[i], sem).start()
        return 0

    lax.fori_loop(0, out.shape[0], start, 0, unroll=True)
    pltpu.make_async_copy(src, out, sem).wait()


def choose(slot_map, pieces):
    return pl.pallas_call(
        choose_kernel,
        out_shape=jax.ShapeDtypeStruct(pieces.shape, BF16),
        in_specs=[smem(), anywhere()],
        out_specs=vmem(),
        scratch_shapes=[pltpu.SemaphoreType.DMA],
        compiler_params=params(16),
        name="choose",
    )(slot_map, pieces)


def fold(rows, chunk, c, boxed):
    tiles = chunk.shape[0]
    members = rows.shape[0] // BOX
    for i in range(tiles):
        chunk[i] = rows[:, i * LANES:(i + 1) * LANES]
        for k in range(PART):
            boxed[k * tiles + i, pl.ds(c, members, stride=BOX), :] = chunk[i, pl.ds(k, members, stride=BOX), :]


def rounded(boxed, out):
    for i in range(boxed.shape[0]):
        out[:, i * LANES:(i + 1) * LANES] = boxed[i].astype(BF16)


def back_kernel(bg_h, gu_h, out, bg, gu, chunk, boxed, done, sem):
    steps, wide = gu.shape[:2]
    load_bg = pltpu.make_async_copy(bg_h, bg, sem.at[0])

    def load(c):
        return pltpu.make_async_copy(gu_h.at[pl.ds(pl.multiple_of(c * wide, wide), wide)], gu.at[c], sem.at[1 + c])

    load_bg.start()
    for c in range(steps):
        load(c).start()
    load_bg.wait()

    def one(c, _):
        load(c).wait()
        fold(lax.dot_general(bg[...], gu[c], NT, preferred_element_type=F32), chunk, c, boxed)
        return 0

    lax.fori_loop(0, steps, one, 0)
    rounded(boxed, done)
    save = pltpu.make_async_copy(done, out, sem.at[1 + steps])
    save.start()
    save.wait()


def folded(members, d):
    wide = d // BOX
    return [
        pltpu.VMEM((wide // LANES, members * BOX, LANES), F32),
        pltpu.VMEM((PART * wide // LANES, members * BOX, LANES), F32),
    ]


def back(members, bg, gate_up):
    slots, f2 = bg.shape
    d = gate_up.shape[0]
    wide = d // BOX
    shape = (members * BOX, PART * wide)
    return pl.pallas_call(
        back_kernel,
        out_shape=pltpu.HBM(shape, BF16),
        in_specs=[anywhere()] * 2,
        out_specs=anywhere(),
        scratch_shapes=[pltpu.VMEM((slots, f2), BF16), pltpu.VMEM((BOX, wide, f2), BF16)] + folded(members, d) + [
            pltpu.VMEM(shape, BF16), pltpu.SemaphoreType.DMA((2 + BOX,)),
        ],
        compiler_params=params(32),
        name="back",
    )(bg, gate_up)


def serve_kernel(scal, blocks_a, blocks_b, x_h, w_a, w_b, out, x, gu, dw, hid, chunk, boxed, sem):
    half = scal[0]
    d = x.shape[1]
    high, f2 = gu.shape[3:]
    f = f2 // 2
    fc = 256
    steps = f2 // fc
    deep = dw.shape[1]
    base = w_a.shape[2] - deep

    load_x = pltpu.make_async_copy(x_h, x, sem.at[0])

    def load_gu(s, n):
        src, place = ((w_a, half), (w_b, 1 - half))[s]
        return pltpu.make_async_copy(
            src.at[:, :, pl.ds(n * high, high), :], gu.at[place, :, :, :, pl.ds(n * fc, fc)], sem.at[1 + 2 * n + s]
        )

    def load_dw(s, n):
        src, place = ((w_a, half), (w_b, 1 - half))[s]
        cols = pl.ds(pl.multiple_of(place * (d // 2) + n * fc, fc), fc)
        return pltpu.make_async_copy(
            src.at[:, n, pl.ds(base, deep), :], dw.at[:, :, cols], sem.at[1 + 2 * steps + 2 * n + s]
        )

    load_x.start()
    for n in range(steps):
        for s in range(2):
            load_gu(s, n).start()
    for n in range(4):
        for s in range(2):
            load_dw(s, n).start()
    load_x.wait()
    kept, scale = kept_and_scale(x[:, :LANES], half, limit_of(1, scal, blocks_a, blocks_b))
    for n in range(steps):
        for s in range(2):
            load_gu(s, n).wait()

    def project(i, _):
        left = pl.ds(pl.multiple_of(i * fc, fc), fc)
        right = pl.ds(pl.multiple_of(f + i * fc, fc), fc)
        g = jnp.dot(x[...], gu[:, :, :, :, left].reshape(d, fc), preferred_element_type=F32)
        u = jnp.dot(x[...], gu[:, :, :, :, right].reshape(d, fc), preferred_element_type=F32)
        hid[:, left] = (g * jax.nn.sigmoid(g) * u).astype(BF16)
        return 0

    lax.fori_loop(0, f // fc, project, 0)
    for n in range(4):
        for s in range(2):
            load_dw(s, n).wait()

    wide = d // BOX

    def outputs(c, _):
        cols = pl.ds(pl.multiple_of(c * wide, wide), wide)
        o = jnp.dot(hid[...], dw[:, :, cols].reshape(f, wide), preferred_element_type=F32)
        fold(jnp.where(kept, scale * o, 0.0), chunk, c, boxed)
        return 0

    lax.fori_loop(0, BOX, outputs, 0)
    rounded(boxed, out)


def serve(members, scal, blocks_a, blocks_b, x, w_a, w_b):
    slots, d = x.shape
    f = d * 3 // 8
    high = d // 2 // 64
    steps = 2 * f // 256
    return pl.pallas_call(
        serve_kernel,
        out_shape=pltpu.HBM((members * BOX, PART * d // BOX), BF16),
        in_specs=[smem(), smem(), smem()] + [anywhere()] * 3,
        out_specs=vmem(),
        scratch_shapes=[
            pltpu.VMEM((slots, d), BF16), pltpu.VMEM((2, 16, 4, high, 2 * f), BF16), pltpu.VMEM((16, f // 16, d), BF16),
            pltpu.VMEM((slots, f), BF16), *folded(members, d), pltpu.SemaphoreType.DMA((9 + 2 * steps,)),
        ],
        compiler_params=params(40),
        name="serve",
    )(scal, blocks_a, blocks_b, x, w_a, w_b)


def unpack_kernel(first, scal, pick, train, serve, given, out, box, wide_box, rows, done, sem):
    half = scal[0]
    parts = 4
    high = box.shape[0] // parts
    wide = box.shape[1] // PART
    members = box.shape[0] // BOX
    tiles = wide // LANES
    pair = rows.shape[1] // wide

    def load(src, i):
        part = pl.ds(i * high, high)
        return pltpu.make_async_copy(src.at[part], box.at[part], sem.at[i])

    def save(c):
        cols = pl.ds(pl.multiple_of(c * pair * wide, wide), pair * wide)
        return pltpu.make_async_copy(done.at[:, cols], out.at[:, cols], sem.at[parts + c])

    @pl.when(half == 0)
    def _():
        for i in range(parts):
            load(train, i).start()

    @pl.when(half == 1)
    def _():
        for i in range(parts):
            load(serve, i).start()

    for i in range(parts):
        load(train, i).wait()
        part = slice(i * high, (i + 1) * high)
        for j in range(wide_box.shape[0]):
            wide_box[j, part, :] = box[part, j * LANES:(j + 1) * LANES].astype(F32)

    def one(c, _):
        cols = pl.ds(pl.multiple_of(c * pair * wide, wide), pair * wide)
        for k in range(PART):
            for i in range(tiles):
                for b in range(pair):
                    lanes = slice((b * tiles + i) * LANES, (b * tiles + i + 1) * LANES)
                    rows[k * members:(k + 1) * members, lanes] = wide_box[
                        k * tiles + i, pl.ds(c * pair + b, members, stride=BOX), :
                    ].astype(BF16)
        total = jnp.dot(pick[...], rows[...], preferred_element_type=F32)
        if not first:
            total = total + given[:, cols].astype(F32)
        done[:, cols] = total.astype(BF16)
        save(c).start()
        return 0

    lax.fori_loop(0, BOX // pair, one, 0, unroll=2)
    for c in range(BOX // pair):
        save(c).wait()


def unpack(scal, pick, train, serve, given=None):
    rows, slots = pick.shape
    wide = train.shape[1] // PART
    d = wide * BOX
    first = given is None
    return pl.pallas_call(
        lambda *refs: unpack_kernel(first, *refs),
        out_shape=jax.ShapeDtypeStruct((rows, d), BF16),
        in_specs=[smem(), vmem(), anywhere(), anywhere(), smem() if first else vmem()],
        out_specs=anywhere(),
        scratch_shapes=[
            pltpu.VMEM(train.shape, BF16), pltpu.VMEM((train.shape[1] // LANES, train.shape[0], LANES), F32),
            pltpu.VMEM((slots, 4 * wide), BF16),
            pltpu.VMEM((rows, d), BF16), pltpu.SemaphoreType.DMA((4 + BOX,)),
        ],
        compiler_params=params(16),
        name="unpack" if first else "unpack_rest",
    )(scal, pick, train, serve, scal if first else given)


def swap(value):
    return lax.ppermute(value, "half", SWAP)


def spread(value):
    return lax.all_to_all(value, "ep", split_axis=0, concat_axis=0, tiled=True)


def step(activations, routes, blocks, row_scale, gate_up, down_weight, slot_map):
    members = lax.axis_size("ep")
    tokens = activations[0]
    row_count, width = tokens.shape
    boxed = (members, BOX, width)
    flat = (members * BOX, width)
    route = routes.reshape(1, row_count)
    gate_up, down_weight = gate_up[0], down_weight[0]
    scal = jnp.stack([lax.axis_index("half"), lax.axis_index("ep")]).astype(jnp.int32)
    eta = 0.03 / math.sqrt(row_count)

    gate_h, down_h = in_hbm(gate_up, down_weight)
    tokens_b = swap(tokens)
    route_b = swap(route)
    scale_b = swap(row_scale)
    blocks_b = swap(blocks)
    train_p, train_i, serve_p, serve_i, own_p, recv_p = prepare(
        members, scal, *in_hbm(route), route_b, *in_hbm(row_scale), scale_b
    )
    tokens_h = in_hbm(tokens)[0]
    packed = pack(0, scal, tokens_h, tokens_b, train_p, train_i)
    train_rows = spread(packed.reshape(boxed)).reshape(flat)
    packed = pack(1, scal, tokens_h, tokens_b, serve_p, serve_i)
    serve_rows = spread(packed.reshape(boxed)).reshape(flat)

    train_rows_b = swap(train_rows)
    hidden, grad_own, grad_send, both = train(scal, blocks, blocks_b, train_rows, gate_h, down_h)
    both_b = swap(both)
    rows_t = turned(scal, train_rows, train_rows_b)
    hidden_send, grad_send, _ = lax.optimization_barrier((hidden, grad_send, both_b))
    hidden_b = swap(hidden_send)
    grad_b = swap(grad_send)
    new = update_gate(eta, scal, rows_t, both, both_b, gate_h)
    new = update_down(eta, scal, hidden, hidden_b, grad_own, grad_b, down_h, new)
    laid = new.shape
    tiled = (members,) + laid[2:]
    pieces = spread(new.reshape(tiled))
    both, _ = lax.optimization_barrier((both, new))
    input_grad = back(members, both, gate_h)
    chosen = choose(slot_map, pieces)
    slots = spread(chosen)
    input_grad, _ = lax.optimization_barrier((input_grad, slots))
    train_back = spread(input_grad.reshape((members, BOX, -1))).reshape(input_grad.shape)
    slots_b = swap(slots)
    served = serve(members, scal, blocks, blocks_b, serve_rows, slots.reshape(laid), slots_b.reshape(laid))
    serve_back = spread(served.reshape((members, BOX, -1))).reshape(served.shape)
    train_other = swap(train_back)
    serve_other = swap(serve_back)
    rows = unpack(scal, own_p, train_back, serve_back)
    return unpack(scal, recv_p, train_other, serve_other, rows)[None]


def solution(mesh):
    placed = (
        P("half", "ep", None),
        P("half", "ep", None),
        P("half", None),
        P("half", "ep"),
        P("ep", None, None),
        P("ep", None, None),
        P(),
    )
    return jax.shard_map(step, mesh=mesh, in_specs=placed, out_specs=P("half", "ep", None), check_vma=False)
```
